128 devices in a mesh: req: 4 (over y), exp: 32 (over z, x, core).
Axes of the slice: x: 4, y: 4, z: 4, core: 2. Of those that a mesh axis runs over, the one named last changes fastest.
Arguments:
- residual: bfloat16 [8192, 2048], P(('req', 'exp')), may hold values from -3 to 3
- q_proj: bfloat16 [8192, 4096], P(('req', 'exp')), may hold values from -6 to 6
- kv_proj: bfloat16 [8192, 1024], P(('req', 'exp')), may hold values from -6 to 6
- q_gain: float32 [128], replicated, may hold values from 0.6 to 8
- k_gain: float32 [128], replicated, may hold values from 0.5 to 1.5
- cache_k: bfloat16 [128, 1024, 512], P(('req', 'exp')), may hold values from -21 to 21
- cache_v: bfloat16 [128, 1024, 512], P(('req', 'exp')), may hold values from -6 to 6
- cache_len: int32 [128], P(('req', 'exp')), may hold values from 8 to 960, as said below
- parents: int32 [128, 64], P(('req', 'exp')), may hold values from -1 to 62, as said below
- accepted_leaf: int32 [128], P(('req', 'exp')), may hold values from 0 to 63
- o_weight: bfloat16 [4096, 2048], P(None, 'req'), may hold values from -0.09375 to 0.09375
- post_gain: float32 [2048], replicated, may hold values from 0.1 to 1.9
- routes: int32 [8192, 8], P(('req', 'exp')), may hold values from 0 to 127, all different within a row; in each aligned block of 64 rows (0 to 63, 64 to 127, ...) at most 8 rows name the same one
- route_gates: float32 [8192, 8], P(('req', 'exp')), may hold values from 0.02 to 1
- w_gate: bfloat16 [128, 2048, 768], P(('req', 'exp')), may hold values from -0.125 to 0.125
- w_up: bfloat16 [128, 2048, 768], P(('req', 'exp')), may hold values from -0.125 to 0.125
- w_down: bfloat16 [128, 768, 2048], P(('req', 'exp')), may hold values from -0.21875 to 0.21875
Outputs:
- hidden_out: bfloat16 [8192, 2048], P(('req', 'exp'))
- new_cache_k: bfloat16 [128, 1024, 512], P(('req', 'exp'))
- new_cache_v: bfloat16 [128, 1024, 512], P(('req', 'exp'))
The draws below stay inside these ranges and needn't reach their ends.
Inputs may be any that keep to these rules, and one draw needn't show every extreme that they name: `cache_len`: some request has exactly 960 cached tokens. parents[r, d] < d; -1 means the draft follows the cached tokens. `routes`: among the rows of one device no expert is named more than 8 times, a bound that some block reaches.
All inputs are finite; a program needn't handle non-finite values.
Results may differ from the reference program's by a relative error of at most 0.015.
Values may be sent and summed in bfloat16 or wider, within the bound.
No kernel may reach another device: no remote copies, remote signals or barrier semaphores. Data moves between devices by JAX's collectives and lax.ppermute only.
A program may use at most 128 MiB of HBM per device.

```python
import math
import jax
import jax.numpy as jnp
import numpy as np
from jax import lax

D = 2048
HEADS = 32
KV_HEADS = 4
HEAD_DIM = 128
FF = 768
TOPK = 8
DRAFT = 64
CAP = 1024
WINDOW = 512
SINKS = 4
EXPERTS = 128
TOK_DEV = 64
REQS = 128
TOKENS = 8192
CAPACITY = 8
N_REQ = 4
N_EXP = 32


def draw_q_gain(key, part):
    return jax.random.uniform(key, (HEAD_DIM,), jnp.float32, 0.6, 1.6)


def draw_cache_k(key, part):
    feature_width = KV_HEADS * HEAD_DIM
    return jnp.clip(jax.random.normal(key, (REQS, CAP, feature_width), jnp.float32), -6.0, 6.0).astype(jnp.bfloat16)


def draw_cache_len(key, part):
    lengths = jax.random.randint(jax.random.fold_in(key, 1), (REQS,), 8, CAP - DRAFT + 1)
    longest = jax.random.randint(jax.random.fold_in(key, 2), (), 0, REQS)
    return jnp.where(jnp.arange(REQS) == longest, CAP - DRAFT, lengths).astype(jnp.int32)


def draw_parents(key, part):
    step_back = jax.random.randint(key, (REQS, DRAFT), 0, 4)
    return jnp.maximum(jnp.arange(DRAFT, dtype=jnp.int32)[None, :] - 1 - step_back, -1).astype(jnp.int32)


def plant(drawn, key, smallest, top_value):
    spot = [jax.random.randint(jax.random.fold_in(key, axis), (), 0, length) for axis, length in enumerate(drawn.shape)]
    widest = drawn.shape.index(max(drawn.shape))
    beside = spot[:widest] + [(spot[widest] + 1) % drawn.shape[widest]] + spot[widest + 1:]
    return drawn.at[tuple(spot)].set(smallest).at[tuple(beside)].set(top_value)


def block_scale(stream_key, shape, pieces, smallest, top_value):
    level, own = 1.0, jax.random.fold_in(stream_key, 6)
    for position, shards_of in pieces:
        steps = jnp.exp(jax.random.uniform(jax.random.fold_in(own, position), (shards_of,), jnp.float32, smallest / len(pieces), top_value / len(pieces)))
        level = level * jnp.repeat(steps, shape[position] // shards_of).reshape([-1 if axis == position else 1 for axis in range(len(shape))])
    return level


def assign_block(own_key, own, number, rows, number_of, top, reach, slope):
    order = jax.random.permutation(own_key, number_of)
    packed, ordinary = portions_of(number_of, rows * top, reach, slope, True), portions_of(number_of, rows * top, reach, slope, False)
    places = jnp.arange(number_of)

    def named(sizes, turn):
        used = int((sizes > 0).sum())
        fixed = max(1, used // 4)
        passed = fixed + (places - fixed + turn * (used - fixed)) % max(1, number_of - fixed)
        return jnp.zeros((number_of,), jnp.int32).at[order[jnp.where(places < fixed, places, passed)]].set(jnp.asarray(sizes, jnp.int32))

    sizes = jnp.where(number % 4 == 0, named(packed, number // 4), named(ordinary, number - number // 4 - 1))
    mixed = jax.random.permutation(jax.random.fold_in(own, 3), number_of)
    source_of, sink = mixed[0:number_of // 2 * 2:2], mixed[1:number_of // 2 * 2:2]
    margin = jnp.minimum(sizes[source_of] - 1, reach - sizes[sink]) // 2
    margin = jnp.where((source_of == order[0]) | (sink == order[0]) | (sizes[sink] == 0), 0, jnp.maximum(margin, 0))
    passed = jax.random.randint(jax.random.fold_in(own, 4), (number_of // 2,), 0, 1 << 20) % (margin + 1)
    sizes = sizes.at[source_of].add(-passed).at[sink].add(passed)
    members = jnp.searchsorted(jnp.cumsum(sizes), jnp.arange(rows * top), side="right").astype(jnp.int32)
    listing = members.reshape(top, rows).T
    listing = listing[jax.random.permutation(jax.random.fold_in(own, 1), rows)]
    turn = jax.random.randint(jax.random.fold_in(own, 2), (rows, 1), 0, top)
    return jnp.take_along_axis(listing, (jnp.arange(top)[None, :] + turn) % top, axis=1)


def portions_of(amount, total, bound, skew, full):
    portions = [(1 << 20) // math.isqrt(rank ** skew) + 1 for rank in range(1, amount + 1)]
    largest = bound if full else min(bound, max(-(-total // amount), total * portions[0] // sum(portions)))
    least = 1 if total - largest >= amount - 1 else 0
    holding, spare = [largest] + [least] * (amount - 1), total - largest - least * (amount - 1)
    while spare > 0:
        movable = [i for i in range(1, amount) if holding[i] < largest] or [i for i in range(1, amount) if holding[i] < bound]
        mass, budget = sum([portions[i] for i in movable]), spare
        for i in movable:
            extra = min(bound - holding[i], max(1, budget * portions[i] // mass), spare)
            holding[i] = holding[i] + extra
            spare = spare - extra
    return np.array(holding)


def gaussian(rng, shape, spread, reach, pieces=(), kind=jnp.bfloat16):
    gain = block_scale(rng, shape, pieces, -0.22, 0.18) if pieces else 1.0
    drawn = jax.random.normal(rng, shape, jnp.float32) * spread * gain
    return jnp.minimum(jnp.maximum(drawn, -reach), reach).astype(kind)


def setup_inputs(seed: int = 0) -> dict:
    key_list = jax.random.split(jax.random.key(seed), 18)
    residual = gaussian(key_list[0], (TOKENS, D), 0.5, 3.0, ((0, 128),))
    q_proj = gaussian(key_list[1], (TOKENS, HEADS * HEAD_DIM), 1.0, 6.0, ((0, 128),))
    kv_proj = gaussian(key_list[2], (TOKENS, 2 * KV_HEADS * HEAD_DIM), 1.0, 6.0, ((0, 128),))
    q_gain = draw_q_gain(jax.random.fold_in(key_list[17], 71), 0)
    k_gain = jnp.clip(jax.random.uniform(key_list[4], (HEAD_DIM,), jnp.float32, 0.5, 1.5), 0.5, 1.5)
    cache_k = draw_cache_k(jax.random.fold_in(key_list[17], 71), 0)
    cache_v = gaussian(key_list[6], (REQS, CAP, KV_HEADS * HEAD_DIM), 1.0, 6.0, ((0, 128),))
    cache_len = draw_cache_len(jax.random.fold_in(key_list[17], 71), 0)
    parents = draw_parents(jax.random.fold_in(key_list[17], 71), 0)
    accepted_leaf = plant(jax.random.randint(key_list[9], (REQS,), 0, DRAFT), jax.random.fold_in(key_list[9], 1), 0, DRAFT - 1).astype(jnp.int32)
    o_weight = gaussian(key_list[10], (HEADS * HEAD_DIM, D), (HEADS * HEAD_DIM) ** -0.5, 0.09375, ((1, 4),))
    post_gain = jnp.clip(1.0 + 0.18 * jax.random.normal(key_list[11], (D,), jnp.float32), 0.1, 1.9)
    routes_keys = jax.random.split(jax.random.fold_in(key_list[12], 1), TOKENS // TOK_DEV)
    routes_turns = jax.random.permutation(jax.random.fold_in(key_list[12], 3), TOKENS // TOK_DEV)
    routes = jax.vmap(lambda own, number: assign_block(jax.random.fold_in(key_list[12], 2), own, number, TOK_DEV, EXPERTS, TOPK, CAPACITY, 2))(routes_keys, routes_turns).reshape((TOKENS, TOPK))
    route_gates = jnp.clip(jnp.exp(math.log(1.0) - 3.912023 * jax.random.uniform(key_list[13], (TOKENS, TOPK), jnp.float32) ** block_scale(key_list[13], (TOKENS, TOPK), ((0, 128),), -0.2, 0.2)), 0.02, 1.0)
    w_gate = gaussian(key_list[14], (EXPERTS, D, FF), D ** -0.5, 0.125, ((0, 128),))
    w_up = gaussian(key_list[15], (EXPERTS, D, FF), D ** -0.5, 0.125, ((0, 128),))
    w_down = gaussian(key_list[16], (EXPERTS, FF, D), FF ** -0.5, 0.21875, ((0, 128),))
    return {"residual": residual, "q_proj": q_proj, "kv_proj": kv_proj, "q_gain": q_gain, "k_gain": k_gain, "cache_k": cache_k, "cache_v": cache_v, "cache_len": cache_len, "parents": parents, "accepted_leaf": accepted_leaf, "o_weight": o_weight, "post_gain": post_gain, "routes": routes, "route_gates": route_gates, "w_gate": w_gate, "w_up": w_up, "w_down": w_down}


ROPE_BASE = 1000000.0
NORM_EPS = 1e-06
MASKED = -1e+30

def ancestry(parent_row):
    count = parent_row.shape[0]
    columns = jnp.arange(count, dtype=jnp.int32)
    linked = (parent_row[:, None] == columns[None, :]).astype(jnp.float32)
    closure = jnp.eye(count, dtype=jnp.float32) + linked
    for squaring in range(count.bit_length()):
        closure = jnp.minimum(jnp.dot(closure, closure, precision=lax.Precision.HIGHEST), 1.0)
    return closure

def rotary(positions, head_dim):
    half_dim = head_dim // 2
    frequency = ROPE_BASE ** (-(jnp.arange(half_dim, dtype=jnp.float32) * 2.0) / head_dim)
    angles = positions[:, None] * frequency[None, :]
    return (jnp.cos(angles), jnp.sin(angles))

def apply_rotary(vectors, cosine_table, sine_table):
    half_dim = vectors.shape[-1] // 2
    lower_half = vectors[..., :half_dim]
    upper_half = vectors[..., half_dim:]
    cos_rows = cosine_table[:, None, :]
    sin_rows = sine_table[:, None, :]
    return jnp.concatenate([lower_half * cos_rows - upper_half * sin_rows, upper_half * cos_rows + lower_half * sin_rows], axis=-1)

def head_norm(vectors, gains):
    return vectors * lax.rsqrt(lax.optimization_barrier(jnp.mean(vectors * vectors, axis=-1, keepdims=True)) + NORM_EPS) * gains

def attend(queries, keyvals, cache_keys, cache_values, length, parent_row, leaf_node, q_gain, k_gain):
    draft_count = queries.shape[0]
    head_dim = q_gain.shape[0]
    slot_count = cache_keys.shape[0]
    group_size = HEADS // KV_HEADS
    closure = ancestry(parent_row)
    depths = lax.optimization_barrier(jnp.sum(closure, axis=1)) - 1.0
    cosine_table, sine_table = rotary(length.astype(jnp.float32) + depths, head_dim)
    query_heads = queries.astype(jnp.float32).reshape(draft_count, HEADS, head_dim)
    query_rot = apply_rotary(head_norm(query_heads, q_gain), cosine_table, sine_table).astype(jnp.bfloat16)
    paired = keyvals.reshape(draft_count, 2, KV_HEADS, head_dim)
    key_rot = apply_rotary(head_norm(paired[:, 0].astype(jnp.float32), k_gain), cosine_table, sine_table).astype(jnp.bfloat16)
    value_new = paired[:, 1]
    key_rows = jnp.concatenate([cache_keys.reshape(slot_count, KV_HEADS, head_dim), key_rot], axis=0)
    value_rows = jnp.concatenate([cache_values.reshape(slot_count, KV_HEADS, head_dim), value_new], axis=0)
    slot_index = jnp.arange(slot_count, dtype=jnp.int32)
    in_cache = (slot_index < length) & ((slot_index < SINKS) | (slot_index >= length - WINDOW))
    visible = jnp.concatenate([jnp.broadcast_to(in_cache[None, :], (draft_count, slot_count)), closure > 0.5], axis=1)
    query_group = query_rot.reshape(draft_count, KV_HEADS, group_size, head_dim)
    scores = jnp.einsum('tgqd,sgd->gtqs', query_group.astype(jnp.float32), key_rows.astype(jnp.float32)) * head_dim ** (-0.5)
    scores = jnp.where(visible[None, :, None, :], scores, MASKED)
    row_max = lax.optimization_barrier(jnp.max(scores, axis=-1, keepdims=True))
    exp_scores = jnp.exp(scores - row_max)
    probs = (exp_scores / lax.optimization_barrier(jnp.sum(exp_scores, axis=-1, keepdims=True))).astype(jnp.bfloat16)
    attended = jnp.einsum('gtqs,sgd->tgqd', probs.astype(jnp.float32), value_rows.astype(jnp.float32))
    attended = attended.astype(jnp.bfloat16).reshape(draft_count, HEADS * head_dim)
    accepted = closure[leaf_node] > 0.5
    target = jnp.where(accepted, length + depths.astype(jnp.int32), slot_count).astype(jnp.int32)
    new_keys = cache_keys.at[target].set(key_rot.reshape(draft_count, KV_HEADS * head_dim), mode='drop')
    new_values = cache_values.at[target].set(value_new.reshape(draft_count, KV_HEADS * head_dim), mode='drop')
    return (attended, new_keys, new_values)

def reference(residual, q_proj, kv_proj, q_gain, k_gain, cache_k, cache_v, cache_len, parents, accepted_leaf, o_weight, post_gain, routes, route_gates, w_gate, w_up, w_down):
    request_count = cache_k.shape[0]

    def per_request(operands):
        queries, keyvals, cache_keys, cache_values, length, parent_row, leaf_node = operands
        return attend(queries, keyvals, cache_keys, cache_values, length, parent_row, leaf_node, q_gain, k_gain)
    attended, new_keys, new_values = lax.map(per_request, (q_proj.reshape(request_count, DRAFT, HEADS * HEAD_DIM), kv_proj.reshape(request_count, DRAFT, 2 * KV_HEADS * HEAD_DIM), cache_k, cache_v, cache_len, parents, accepted_leaf))
    attended = attended.reshape(TOKENS, HEADS * HEAD_DIM)
    projected = jnp.dot(attended, o_weight, preferred_element_type=jnp.float32)
    middle = (residual.astype(jnp.float32) + projected).astype(jnp.bfloat16)
    middle32 = middle.astype(jnp.float32)
    normed = (middle32 * lax.rsqrt(lax.optimization_barrier(jnp.mean(middle32 * middle32, axis=-1, keepdims=True)) + NORM_EPS) * post_gain).astype(jnp.bfloat16)
    source_count = N_REQ * N_EXP
    expert_count = w_gate.shape[0]
    top_count = routes.shape[1]
    assign_count = TOK_DEV * top_count
    route_block = routes.reshape(source_count, assign_count)

    def slot_ranks(block_row):
        onehot = (block_row[:, None] == jnp.arange(expert_count, dtype=jnp.int32)[None, :]).astype(jnp.int32)
        return lax.optimization_barrier(jnp.sum((jnp.cumsum(onehot, axis=0) - onehot) * onehot, axis=1))
    slot_rank = jax.vmap(slot_ranks)(route_block).astype(jnp.int32)
    source_ids = jnp.broadcast_to(jnp.arange(source_count, dtype=jnp.int32)[:, None], (source_count, assign_count))
    token_ids = source_ids * TOK_DEV + jnp.arange(assign_count, dtype=jnp.int32)[None, :] // top_count
    row_table = jnp.full((expert_count, source_count, CAPACITY), -1, jnp.int32).at[route_block, source_ids, slot_rank].set(token_ids)

    def expert_rows(operands):
        table_rows, gate_weight, up_weight, down_weight = operands
        flat_index = table_rows.reshape(-1)
        gathered = jnp.where((flat_index >= 0)[:, None], normed[jnp.maximum(flat_index, 0)], jnp.zeros((), normed.dtype))
        gate_act = jnp.dot(gathered, gate_weight, preferred_element_type=jnp.float32)
        up_act = jnp.dot(gathered, up_weight, preferred_element_type=jnp.float32)
        hidden = (jax.nn.silu(gate_act) * up_act).astype(jnp.bfloat16)
        return jnp.dot(hidden, down_weight, preferred_element_type=jnp.float32).astype(jnp.bfloat16)
    expert_out = lax.map(expert_rows, (row_table, w_gate, w_up, w_down))
    picked = expert_out[route_block, source_ids * CAPACITY + slot_rank].reshape(TOKENS, top_count, D)
    mixture = lax.optimization_barrier(jnp.sum(picked.astype(jnp.float32) * route_gates[:, :, None], axis=1))
    hidden_out = (middle.astype(jnp.float32) + mixture).astype(jnp.bfloat16)
    return (hidden_out, new_keys, new_values)
```

```python
import functools

import jax
import jax.numpy as jnp
import numpy as np
from jax import lax
from jax.experimental import pallas as pl
from jax.experimental.pallas import tpu as pltpu
from jax.sharding import PartitionSpec as P

HEADS = 32
KV_HEADS = 4
WINDOW = 512
SINKS = 4

ROPE_BASE = 1000000.0
NORM_EPS = 1e-06
MASKED = -1e30

F32 = jnp.float32
BF16 = jnp.bfloat16


def matmul(a, b):
    return jnp.dot(a, b, preferred_element_type=F32)


def contract(a, b, dims_a, dims_b):
    return lax.dot_general(a, b, (((dims_a,), (dims_b,)), ((), ())), preferred_element_type=F32)


def iota(shape, axis):
    return lax.broadcasted_iota(jnp.int32, shape, axis)


def attention_kernel(
    span,
    length_ref,
    leaf_ref,
    parents_ref,
    freq_ref,
    q_gain_ref,
    k_gain_ref,
    q_ref,
    k_ref,
    v_ref,
    cache_k_ref,
    cache_v_ref,
    out_ref,
    new_k_ref,
    new_v_ref,
    cos_ref,
    sin_ref,
    tree_ref,
    place_ref,
):
    draft = k_ref.shape[0]
    width = k_ref.shape[1]
    slots = cache_k_ref.shape[0]
    group = q_ref.shape[1] // width
    length = length_ref[0]
    patch = draft + 16
    patch_at = pl.multiple_of(jnp.minimum(length // 16 * 16, slots - patch), 16)

    @pl.when(pl.program_id(0) == 0)
    def _():
        child = iota((draft, draft), 1)
        node = iota((draft, draft), 0)
        eye = (child == node).astype(F32)
        links = eye + (parents_ref[...] == node).astype(F32)
        links = links.astype(BF16)
        for _ in range((draft - 1).bit_length()):
            links = jnp.minimum(matmul(links, links), 1.0).astype(BF16)
        closure = contract(links, eye.astype(BF16), 0, 0)
        depth = jnp.sum(closure, axis=1, keepdims=True) - 1.0
        angle = (length.astype(F32) + depth) * freq_ref[...]
        cosine = jnp.cos(angle)
        sine = jnp.sin(angle)
        lane = iota((draft, width), 1)
        cos_ref[...] = cosine
        sin_ref[...] = jnp.where(lane < width // 2, -sine, sine)
        tree_ref[:, :draft] = jnp.where(closure > 0.5, 0.0, MASKED)
        head = iota((draft, width - draft), 1)
        first = jnp.maximum(length - WINDOW, 0) // 16 * 16
        first = jnp.minimum(first, slots - span)
        seen = (head < SINKS) & (head < length) & (head < first)
        tree_ref[:, draft:] = jnp.where(seen, 0.0, MASKED)
        chosen = (iota((8, draft), 1) == leaf_ref[0]).astype(BF16)
        accepted = matmul(chosen, closure.astype(BF16))[:1]
        depths = contract(jnp.ones((8, draft), BF16), closure.astype(BF16), 1, 1)[:1] - 1.0
        row = iota((patch, draft), 0) + patch_at - length
        place_ref[...] = ((row == depths.astype(jnp.int32)) & (accepted > 0.5)).astype(BF16)

    cosine = cos_ref[...]
    sine = sin_ref[...]

    def turned(x, gain):
        x = x * lax.rsqrt(jnp.mean(x * x, axis=-1, keepdims=True) + NORM_EPS) * gain
        return x, pltpu.roll(x, width // 2, axis=1)

    k_new, k_swapped = turned(k_ref[...].astype(F32), k_gain_ref[...])
    k_new = (k_new * cosine + k_swapped * sine).astype(BF16)
    v_new = v_ref[...]
    queries = q_ref[...].astype(F32)
    queries = jnp.concatenate(
        [queries[:, h * width : (h + 1) * width] for h in range(group)], axis=0
    )
    queries, q_swapped = turned(queries, q_gain_ref[...])
    shape = (group, draft, width)
    queries = (
        queries.reshape(shape) * cosine[None] + q_swapped.reshape(shape) * sine[None]
    ).reshape(group * draft, width).astype(BF16)

    first = jnp.minimum(jnp.maximum(length - WINDOW, 0) // 16 * 16, slots - span)
    first = pl.multiple_of(first, 16)
    pad = jnp.zeros((width - draft - 16, width), BF16)
    keys = cache_k_ref[pl.ds(first, span), :]
    values = cache_v_ref[pl.ds(first, span), :]
    own_keys = jnp.concatenate([k_new, cache_k_ref[:16, :], pad], axis=0)
    own_values = jnp.concatenate([v_new, cache_v_ref[:16, :], pad], axis=0)
    slot = iota((1, span), 1) + first
    seen = (slot < length) & ((slot < SINKS) | (slot >= length - WINDOW))
    far = contract(queries, keys, 1, 1) + jnp.where(seen, 0.0, MASKED)
    near = contract(queries, own_keys, 1, 1).reshape(shape) + tree_ref[...][None]
    near = near.reshape(group * draft, width)
    top = jnp.maximum(
        jnp.max(far, axis=-1, keepdims=True), jnp.max(near, axis=-1, keepdims=True)
    )
    scale = float(width) ** -0.5 * float(np.log2(np.e))
    far = jnp.exp2((far - top) * scale)
    near = jnp.exp2((near - top) * scale)
    total = jnp.sum(far, axis=-1, keepdims=True) + jnp.sum(near, axis=-1, keepdims=True)
    mixed = matmul(far.astype(BF16), values) + matmul(near.astype(BF16), own_values)
    mixed = (mixed / total).astype(BF16)
    for h in range(group):
        out_ref[:, h * width : (h + 1) * width] = mixed[h * draft : (h + 1) * draft]

    place = place_ref[...]
    taken = jnp.sum(place.astype(F32), axis=1, keepdims=True) > 0.5
    rows = pl.ds(patch_at, patch)
    for cache_ref, new_ref, fresh in (
        (cache_k_ref, new_k_ref, k_new),
        (cache_v_ref, new_v_ref, v_new),
    ):
        new_ref[...] = cache_ref[...]
        put = matmul(place, fresh).astype(BF16)
        new_ref[rows, :] = jnp.where(taken, put, cache_ref[rows, :])


def attention(q_proj, kv_proj, q_gain, k_gain, cache_k, cache_v, length, parents, leaf):
    draft = q_proj.shape[0]
    width = q_gain.shape[0]
    slots = cache_k.shape[0]
    span = min(slots, WINDOW + 128)
    half = width // 2
    freq = ROPE_BASE ** (-(np.arange(half) * 2.0) / width)
    freq = jnp.asarray(np.concatenate([freq, freq])[None, :], F32)
    per_group = HEADS // KV_HEADS * width
    smem = pl.BlockSpec(memory_space=pltpu.SMEM)
    whole = lambda shape: pl.BlockSpec(shape, lambda g: (0, 0))
    return pl.pallas_call(
        functools.partial(attention_kernel, span),
        grid=(KV_HEADS,),
        in_specs=[
            smem,
            smem,
            whole((1, draft)),
            whole((1, width)),
            whole((1, width)),
            whole((1, width)),
            pl.BlockSpec((draft, per_group), lambda g: (0, g)),
            pl.BlockSpec((draft, width), lambda g: (0, g)),
            pl.BlockSpec((draft, width), lambda g: (0, g + KV_HEADS)),
            pl.BlockSpec((slots, width), lambda g: (0, g)),
            pl.BlockSpec((slots, width), lambda g: (0, g)),
        ],
        out_specs=[
            pl.BlockSpec((draft, per_group), lambda g: (0, g)),
            pl.BlockSpec((slots, width), lambda g: (0, g)),
            pl.BlockSpec((slots, width), lambda g: (0, g)),
        ],
        out_shape=[
            jax.ShapeDtypeStruct(q_proj.shape, BF16),
            jax.ShapeDtypeStruct(cache_k.shape, BF16),
            jax.ShapeDtypeStruct(cache_v.shape, BF16),
        ],
        scratch_shapes=[
            pltpu.VMEM((draft, width), F32),
            pltpu.VMEM((draft, width), F32),
            pltpu.VMEM((draft, width), F32),
            pltpu.VMEM((draft + 16, draft), BF16),
        ],
        name="attention",
        cost_estimate=pl.CostEstimate(
            flops=2 * 2 * HEADS * draft * (span + width) * width,
            bytes_accessed=6 << 20,
            transcendentals=HEADS * draft * (span + width),
        ),
    )(
        length,
        leaf,
        parents,
        freq,
        q_gain[None],
        k_gain[None],
        q_proj,
        kv_proj,
        kv_proj,
        cache_k,
        cache_v,
    )


def dispatch_kernel(
    at_ref, p0_ref, p1_ref, p2_ref, p3_ref, residual_ref, gain_ref, slot_ref, middle_ref, *rest
):
    outs, (normed_ref,) = rest[:-1], rest[-1:]
    step = pl.program_id(0)
    rows = outs[0].shape[0]

    @pl.when(step == 0)
    def _():
        at = at_ref[0]
        pieces = (p0_ref, p1_ref, p2_ref, p3_ref)
        count = len(pieces)
        cols = p0_ref.shape[1]
        for j in range(count):
            own = lax.rem(j - at + count, count)
            piece = pieces[0][...].astype(F32)
            for s in range(1, count):
                piece = jnp.where(own == s, pieces[s][...].astype(F32), piece)
            block = pl.ds(j * cols, cols)
            middle_ref[:, block] = (residual_ref[:, block].astype(F32) + piece).astype(BF16)
        middle = middle_ref[...].astype(F32)
        power = jnp.mean(middle * middle, axis=-1, keepdims=True)
        normed_ref[...] = (middle * lax.rsqrt(power + NORM_EPS) * gain_ref[...]).astype(BF16)

    tokens = normed_ref.shape[0]
    row = iota((rows, tokens), 0) + step * rows
    pick = row == slot_ref[0:1, :]
    for k in range(1, slot_ref.shape[0]):
        pick = pick | (row == slot_ref[k : k + 1, :])
    pick = pick.astype(F32).astype(BF16)
    cols = outs[0].shape[1]
    for j, out_ref in enumerate(outs):
        out_ref[...] = matmul(pick, normed_ref[:, j * cols : (j + 1) * cols]).astype(BF16)


def dispatch(at, pieces, residual, gain, slots_t, slot_count, chunks):
    tokens, width = residual.shape
    steps = 4
    cols = width // chunks
    rows = slot_count // steps
    whole = lambda x: pl.BlockSpec(x.shape, lambda i: (0, 0))
    return pl.pallas_call(
        dispatch_kernel,
        grid=(steps,),
        in_specs=[pl.BlockSpec(memory_space=pltpu.SMEM)]
        + [whole(p) for p in pieces]
        + [whole(residual), whole(gain), whole(slots_t)],
        out_specs=[whole(residual)]
        + [pl.BlockSpec((rows, cols), lambda i: (i, 0)) for _ in range(chunks)],
        out_shape=[jax.ShapeDtypeStruct(residual.shape, BF16)]
        + [jax.ShapeDtypeStruct((slot_count, cols), BF16) for _ in range(chunks)],
        scratch_shapes=[pltpu.VMEM((tokens, width), BF16)],
        name="dispatch",
        cost_estimate=pl.CostEstimate(
            flops=2 * slot_count * tokens * width,
            bytes_accessed=2 * slot_count * width,
            transcendentals=0,
        ),
    )(at, *pieces, residual, gain, slots_t)


def first_kernel(x_ref, gate_ref, up_ref, gate_out, up_out):
    x = x_ref[...]
    gate_out[...] = matmul(x, gate_ref[...])
    up_out[...] = matmul(x, up_ref[...])


def second_kernel(
    x_ref, gate_ref, up_ref, down_ref, gate_in, up_in, hidden_out, first_out
):
    x = x_ref[...]
    gate = matmul(x, gate_ref[...]) + gate_in[...]
    up = matmul(x, up_ref[...]) + up_in[...]
    hidden = (gate / (1.0 + jnp.exp(-gate)) * up).astype(BF16)
    hidden_out[...] = hidden
    first_out[...] = matmul(hidden, down_ref[...]).astype(BF16)


def down_kernel(hidden_ref, down_ref, out_ref):
    out_ref[...] = matmul(hidden_ref[...], down_ref[...]).astype(BF16)


ROWS = 256


def by_rows(cols):
    return pl.BlockSpec((ROWS, cols), lambda i: (i, 0))


def experts(arrived, w_gate, w_up, w_down):
    count = arrived[0].shape[0]
    cols = arrived[0].shape[1]
    width, hidden_width = w_gate.shape
    steps = count // ROWS
    once = pl.Buffered(1)
    part = lambda j: pl.BlockSpec((cols, hidden_width), lambda i: (j, 0), pipeline_mode=once)
    down = lambda j: pl.BlockSpec((hidden_width, cols), lambda i: (0, j), pipeline_mode=once)
    partial_shape = jax.ShapeDtypeStruct((count, hidden_width), F32)
    sent = jax.ShapeDtypeStruct((count, cols), BF16)
    step_flops = 2 * count * cols * hidden_width
    gate, up = pl.pallas_call(
        first_kernel,
        grid=(steps,),
        in_specs=[by_rows(cols), part(0), part(0)],
        out_specs=[by_rows(hidden_width)] * 2,
        out_shape=[partial_shape] * 2,
        name="experts_first",
        cost_estimate=pl.CostEstimate(
            flops=2 * step_flops, bytes_accessed=12 << 20, transcendentals=0
        ),
    )(arrived[0], w_gate, w_up)
    hidden, out0 = pl.pallas_call(
        second_kernel,
        grid=(steps,),
        in_specs=[by_rows(cols), part(1), part(1), down(0)] + [by_rows(hidden_width)] * 2,
        out_specs=[by_rows(hidden_width), by_rows(cols)],
        out_shape=[jax.ShapeDtypeStruct((count, hidden_width), BF16), sent],
        name="experts_second",
        cost_estimate=pl.CostEstimate(
            flops=3 * step_flops, bytes_accessed=16 << 20, transcendentals=count * hidden_width
        ),
    )(arrived[1], w_gate, w_up, w_down, gate, up)
    out1 = pl.pallas_call(
        down_kernel,
        grid=(steps,),
        in_specs=[by_rows(hidden_width), down(1)],
        out_specs=by_rows(cols),
        out_shape=sent,
        name="experts_third",
        cost_estimate=pl.CostEstimate(
            flops=step_flops, bytes_accessed=5 << 20, transcendentals=0
        ),
    )(hidden, w_down)
    return out0, out1


def combine_kernel(part, slot_ref, gates_ref, middle_ref, returned_ref, *rest):
    out_ref = rest[-1]
    tokens, choices = slot_ref.shape
    count = returned_ref.shape[0]
    lane = iota((tokens, count), 1)
    mix = jnp.zeros((tokens, count), F32)
    for k in range(choices):
        mix = jnp.where(lane == slot_ref[:, k : k + 1], gates_ref[:, k : k + 1], mix)
    high = mix.astype(BF16)
    low = (mix - high.astype(F32)).astype(BF16)
    returned = returned_ref[...]
    mixture = matmul(high, returned) + matmul(low, returned)
    out_ref[...] = (middle_ref[...].astype(F32) + mixture).astype(BF16)


def combine(part, slots, gates, middle, returned, filled=None):
    count, cols = returned.shape
    steps = 2
    block = cols // steps
    at = lambda i: (0, part * steps + i)
    whole = lambda x: pl.BlockSpec(x.shape, lambda i: (0, 0))
    tokens = middle.shape[0]
    extra = [] if filled is None else [filled]
    return pl.pallas_call(
        functools.partial(combine_kernel, part),
        grid=(steps,),
        in_specs=[
            whole(slots),
            whole(gates),
            pl.BlockSpec((tokens, block), at),
            pl.BlockSpec((count, block), lambda i: (0, i)),
        ]
        + [pl.BlockSpec(memory_space=pl.ANY) for _ in extra],
        out_specs=pl.BlockSpec((tokens, block), at),
        out_shape=jax.ShapeDtypeStruct(middle.shape, BF16),
        input_output_aliases={4: 0} if extra else {},
        name=f"combine_{part}",
        cost_estimate=pl.CostEstimate(
            flops=4 * tokens * count * cols,
            bytes_accessed=2 * count * cols,
            transcendentals=0,
        ),
    )(slots, gates, middle, returned, *extra)


def slot_table(routes, expert_count, capacity):
    tokens = routes.shape[0]
    onehot = routes[:, :, None] == jnp.arange(expert_count, dtype=jnp.int32)[None, None, :]
    used = jnp.any(onehot, axis=1).astype(BF16)
    earlier = jnp.asarray(np.tril(np.ones((tokens, tokens)), -1), BF16)
    rank = matmul(earlier, used)
    rank = jnp.sum(jnp.where(onehot, rank[:, None, :], 0.0), axis=2).astype(jnp.int32)
    return routes * capacity + rank


def shift(x, by, size):
    return lax.ppermute(x, "req", [(i, (i + by) % size) for i in range(size)])


def shards(
    residual,
    q_proj,
    kv_proj,
    q_gain,
    k_gain,
    cache_k,
    cache_v,
    cache_len,
    parents,
    accepted_leaf,
    o_weight,
    post_gain,
    routes,
    route_gates,
    w_gate,
    w_up,
    w_down,
):
    tok_rows, model_width = residual.shape
    req_size = lax.axis_size("req")
    exp_size = lax.axis_size("exp")
    expert_count = req_size * exp_size
    top_count = routes.shape[1]
    capacity = max(2, 2 * tok_rows * top_count // expert_count)
    chunks = 2

    attended, new_keys, new_values = attention(
        q_proj,
        kv_proj,
        q_gain,
        k_gain,
        cache_k[0],
        cache_v[0],
        cache_len,
        parents,
        accepted_leaf,
    )
    slots = slot_table(routes, expert_count, capacity)
    slots_t = slots.T

    pieces = [matmul(attended, o_weight).astype(BF16)]
    for by in range(1, req_size):
        theirs = shift(attended, -by, req_size)
        product = matmul(theirs, o_weight).astype(BF16)
        pieces.append((by, product))
    pieces = [pieces[0]] + [shift(product, by, req_size) for by, product in pieces[1:]]
    pieces = [pieces[0]] + pieces[:0:-1]

    at = lax.axis_index("req").astype(jnp.int32)[None]
    middle, *outbox = dispatch(
        at, pieces, residual, post_gain[None], slots_t, expert_count * capacity, chunks
    )
    swap = lambda x: lax.all_to_all(
        x.reshape(expert_count, capacity, -1),
        ("req", "exp"),
        split_axis=0,
        concat_axis=0,
        tiled=True,
    ).reshape(expert_count * capacity, -1)
    arrived = [swap(x) for x in outbox]
    outs = experts(arrived, w_gate[0], w_up[0], w_down[0])
    returned = [swap(x) for x in outs]
    hidden_out = combine(0, slots, route_gates, middle, returned[0])
    hidden_out = combine(1, slots, route_gates, middle, returned[1], hidden_out)
    return (hidden_out, new_keys[None], new_values[None])


def solution(mesh):
    placed = (
        P(("req", "exp"), None),
        P(("req", "exp"), None),
        P(("req", "exp"), None),
        P(),
        P(),
        P(("req", "exp"), None, None),
        P(("req", "exp"), None, None),
        P(("req", "exp")),
        P(("req", "exp"), None),
        P(("req", "exp")),
        P(None, "req"),
        P(),
        P(("req", "exp"), None),
        P(("req", "exp"), None),
        P(("req", "exp"), None, None),
        P(("req", "exp"), None, None),
        P(("req", "exp"), None, None),
    )
    return jax.shard_map(
        shards,
        mesh=mesh,
        in_specs=placed,
        out_specs=(
            P(("req", "exp"), None),
            P(("req", "exp"), None, None),
            P(("req", "exp"), None, None),
        ),
        check_vma=False,
    )
```

```python
import functools

import jax
import jax.numpy as jnp
import numpy as np
from jax import lax
from jax.experimental import pallas as pl
from jax.experimental.pallas import tpu as pltpu
from jax.sharding import PartitionSpec as P

HEADS = 32
KV_HEADS = 4
WINDOW = 512
SINKS = 4

ROPE_BASE = 1000000.0
NORM_EPS = 1e-06
MASKED = -1e30

F32 = jnp.float32
BF16 = jnp.bfloat16


def matmul(a, b):
    return jnp.dot(a, b, preferred_element_type=F32)


def contract(a, b, dims_a, dims_b):
    return lax.dot_general(a, b, (((dims_a,), (dims_b,)), ((), ())), preferred_element_type=F32)


def iota(shape, axis):
    return lax.broadcasted_iota(jnp.int32, shape, axis)


def tables(length, leaf, parents_ref, freq_ref, span, slots, patch):
    draft = parents_ref.shape[1]
    width = freq_ref.shape[1]
    child = iota((draft, draft), 1)
    node = iota((draft, draft), 0)
    eye = (child == node).astype(F32)
    links = (eye + (parents_ref[...] == node).astype(F32)).astype(BF16)
    for _ in range((draft - 1).bit_length()):
        links = jnp.minimum(matmul(links, links), 1.0).astype(BF16)
    closure = contract(links, eye.astype(BF16), 0, 0)
    depth = jnp.sum(closure, axis=1, keepdims=True) - 1.0
    angle = (length.astype(F32) + depth) * freq_ref[...]
    sine = jnp.sin(angle)
    sine = jnp.where(iota((draft, width), 1) < width // 2, -sine, sine)
    head = iota((draft, width - draft), 1)
    first = jnp.minimum(jnp.maximum(length - WINDOW, 0) // 16 * 16, slots - span)
    seen = (head < SINKS) & (head < length) & (head < first)
    tree = jnp.concatenate(
        [jnp.where(closure > 0.5, 0.0, MASKED), jnp.where(seen, 0.0, MASKED)], axis=1
    )
    chosen = (iota((8, draft), 1) == leaf).astype(BF16)
    accepted = matmul(chosen, closure.astype(BF16))[:1]
    depths = contract(jnp.ones((8, draft), BF16), closure.astype(BF16), 1, 1)[:1] - 1.0
    row = iota((patch, draft), 0) + patch_start(length, slots, patch) - length
    place = ((row == depths.astype(jnp.int32)) & (accepted > 0.5)).astype(BF16)
    return jnp.cos(angle), sine, tree, place


def patch_start(length, slots, patch):
    return jnp.minimum(length // 16 * 16, slots - patch)


def attention_kernel(opening, span, *refs):
    length_ref, leaf_ref, q_gain_ref, k_gain_ref, q_ref, k_ref, v_ref, cache_k_ref, cache_v_ref = refs[:9]
    refs = refs[9:]
    if opening:
        parents_ref, freq_ref, out_ref, key_ref, cos_ref, sin_ref, tree_ref, place_ref = refs
    else:
        cos_ref, sin_ref, tree_ref, out_ref, key_ref = refs
    draft = k_ref.shape[0]
    width = k_ref.shape[1]
    slots = cache_k_ref.shape[0]
    group = q_ref.shape[1] // width
    length = length_ref[0]

    if opening:

        @pl.when(pl.program_id(0) == 0)
        def _():
            made = tables(
                length, leaf_ref[0], parents_ref, freq_ref, span, slots, place_ref.shape[0]
            )
            for ref, table in zip((cos_ref, sin_ref, tree_ref, place_ref), made):
                ref[...] = table

    cosine = cos_ref[...]
    sine = sin_ref[...]

    def turned(x, gain):
        x = x * lax.rsqrt(jnp.mean(x * x, axis=-1, keepdims=True) + NORM_EPS) * gain
        return x, pltpu.roll(x, width // 2, axis=1)

    k_new, k_swapped = turned(k_ref[...].astype(F32), k_gain_ref[...])
    k_new = (k_new * cosine + k_swapped * sine).astype(BF16)
    key_ref[...] = k_new
    queries = q_ref[...].astype(F32)
    queries = jnp.concatenate(
        [queries[:, h * width : (h + 1) * width] for h in range(group)], axis=0
    )
    queries, q_swapped = turned(queries, q_gain_ref[...])
    shape = (group, draft, width)
    queries = (
        queries.reshape(shape) * cosine[None] + q_swapped.reshape(shape) * sine[None]
    ).reshape(group * draft, width).astype(BF16)

    first = jnp.minimum(jnp.maximum(length - WINDOW, 0) // 16 * 16, slots - span)
    first = pl.multiple_of(first, 16)
    pad = jnp.zeros((width - draft - 16, width), BF16)
    keys = cache_k_ref[pl.ds(first, span), :]
    values = cache_v_ref[pl.ds(first, span), :]
    own_keys = jnp.concatenate([k_new, cache_k_ref[:16, :], pad], axis=0)
    own_values = jnp.concatenate([v_ref[...], cache_v_ref[:16, :], pad], axis=0)
    slot = iota((1, span), 1) + first
    seen = (slot < length) & ((slot < SINKS) | (slot >= length - WINDOW))
    far = contract(queries, keys, 1, 1) + jnp.where(seen, 0.0, MASKED)
    near = contract(queries, own_keys, 1, 1).reshape(shape) + tree_ref[...][None]
    near = near.reshape(group * draft, width)
    top = jnp.maximum(
        jnp.max(far, axis=-1, keepdims=True), jnp.max(near, axis=-1, keepdims=True)
    )
    scale = float(width) ** -0.5 * float(np.log2(np.e))
    far = jnp.exp2((far - top) * scale)
    near = jnp.exp2((near - top) * scale)
    total = jnp.sum(far, axis=-1, keepdims=True) + jnp.sum(near, axis=-1, keepdims=True)
    mixed = matmul(far.astype(BF16), values) + matmul(near.astype(BF16), own_values)
    mixed = (mixed / total).astype(BF16)
    for h in range(group):
        out_ref[:, h * width : (h + 1) * width] = mixed[h * draft : (h + 1) * draft]


def attention(length, leaf, parents, q_gain, k_gain, q_proj, kv_proj, cache_k, cache_v, at, made):
    draft = q_proj.shape[0]
    width = q_gain.shape[0]
    slots = cache_k.shape[0]
    span = min(slots, WINDOW + 128)
    per_group = HEADS // KV_HEADS * width
    groups = KV_HEADS // 2
    base = at * groups
    smem = pl.BlockSpec(memory_space=pltpu.SMEM)
    whole = lambda shape: pl.BlockSpec(shape, lambda g: (0, 0))
    table = jax.ShapeDtypeStruct((draft, width), F32)
    patch = draft + 16
    tables_shape = [table] * 3 + [jax.ShapeDtypeStruct((patch, draft), BF16)]
    in_specs = [
        smem,
        smem,
        whole((1, width)),
        whole((1, width)),
        pl.BlockSpec((draft, per_group), lambda g: (0, g + base)),
        pl.BlockSpec((draft, width), lambda g: (0, g + base)),
        pl.BlockSpec((draft, width), lambda g: (0, g + base + KV_HEADS)),
        pl.BlockSpec((slots, width), lambda g: (0, g + base)),
        pl.BlockSpec((slots, width), lambda g: (0, g + base)),
    ]
    out_specs = [
        pl.BlockSpec((draft, per_group), lambda g: (0, g)),
        pl.BlockSpec((draft, width), lambda g: (0, g)),
    ]
    out_shape = [
        jax.ShapeDtypeStruct((draft, per_group * groups), BF16),
        jax.ShapeDtypeStruct((draft, width * groups), BF16),
    ]
    operands = [length, leaf, q_gain[None], k_gain[None], q_proj, kv_proj, kv_proj, cache_k, cache_v]
    if made is None:
        half = width // 2
        freq = ROPE_BASE ** (-(np.arange(half) * 2.0) / width)
        freq = jnp.asarray(np.concatenate([freq, freq])[None, :], F32)
        operands += [parents, freq]
        in_specs += [whole((1, draft)), whole((1, width))]
        out_specs += [whole(t.shape) for t in tables_shape]
        out_shape += tables_shape
    else:
        operands += made[:3]
        in_specs += [whole(t.shape) for t in made[:3]]
    return pl.pallas_call(
        functools.partial(attention_kernel, made is None, span),
        grid=(groups,),
        in_specs=in_specs,
        out_specs=out_specs,
        out_shape=out_shape,
        name=f"attention_{at}",
        cost_estimate=pl.CostEstimate(
            flops=2 * HEADS * draft * (span + width) * width,
            bytes_accessed=2 << 20,
            transcendentals=HEADS // 2 * draft * (span + width),
        ),
    )(*operands)


def append_kernel(length_ref, place_ref, v_ref, key_a_ref, key_b_ref, cache_k_ref, cache_v_ref, new_k_ref, new_v_ref):
    patch = place_ref.shape[0]
    slots = cache_k_ref.shape[0]
    at = pl.multiple_of(patch_start(length_ref[0], slots, patch), 16)
    place = place_ref[...]
    taken = jnp.sum(place.astype(F32), axis=1, keepdims=True) > 0.5
    rows = pl.ds(at, patch)
    keys = jnp.where(pl.program_id(0) == 0, key_a_ref[...], key_b_ref[...])
    for cache_ref, new_ref, fresh in (
        (cache_k_ref, new_k_ref, keys),
        (cache_v_ref, new_v_ref, v_ref[...]),
    ):
        new_ref[...] = cache_ref[...]
        put = matmul(place, fresh).astype(BF16)
        new_ref[rows, :] = jnp.where(taken, put, cache_ref[rows, :])


def append(length, place, kv_proj, keys, cache_k, cache_v):
    draft, cols = keys[0].shape
    slots = cache_k.shape[0]
    whole = lambda x: pl.BlockSpec(x.shape, lambda g: (0, 0))
    cache_spec = pl.BlockSpec((slots, cols), lambda g: (0, g))
    return pl.pallas_call(
        append_kernel,
        grid=(2,),
        in_specs=[
            pl.BlockSpec(memory_space=pltpu.SMEM),
            whole(place),
            pl.BlockSpec((draft, cols), lambda g: (0, g + 2)),
            whole(keys[0]),
            whole(keys[1]),
            cache_spec,
            cache_spec,
        ],
        out_specs=[cache_spec] * 2,
        out_shape=[
            jax.ShapeDtypeStruct(cache_k.shape, BF16),
            jax.ShapeDtypeStruct(cache_v.shape, BF16),
        ],
        name="append",
        cost_estimate=pl.CostEstimate(
            flops=4 * place.shape[0] * draft * cols * 2,
            bytes_accessed=8 * slots * cols,
            transcendentals=0,
        ),
    )(length, place, kv_proj, *keys, cache_k, cache_v)


def slot_table(routes, expert_count, capacity):
    tokens = routes.shape[0]
    onehot = routes[:, :, None] == jnp.arange(expert_count, dtype=jnp.int32)[None, None, :]
    used = jnp.any(onehot, axis=1).astype(BF16)
    earlier = jnp.asarray(np.tril(np.ones((tokens, tokens)), -1), BF16)
    rank = matmul(earlier, used)
    rank = jnp.sum(jnp.where(onehot, rank[:, None, :], 0.0), axis=2).astype(jnp.int32)
    return routes * capacity + rank


def gather_plan(slots, gates, slot_count):
    index = jnp.arange(slot_count, dtype=jnp.int32)
    slots_t = slots.T
    pick = index[:, None] == slots_t[0][None, :]
    mix = jnp.where(index[None, :] == slots[:, :1], gates[:, :1], 0.0)
    for k in range(1, slots.shape[1]):
        pick = pick | (index[:, None] == slots_t[k][None, :])
        mix = jnp.where(index[None, :] == slots[:, k : k + 1], gates[:, k : k + 1], mix)
    high = lax.reduce_precision(mix, 8, 7)
    return pick.astype(BF16), jnp.concatenate([high, mix - high], axis=0).astype(BF16)


def shift(x, by, size):
    return lax.ppermute(x, "req", [(i, (i + by) % size) for i in range(size)])


def shards(
    residual,
    q_proj,
    kv_proj,
    q_gain,
    k_gain,
    cache_k,
    cache_v,
    cache_len,
    parents,
    accepted_leaf,
    o_weight,
    post_gain,
    routes,
    route_gates,
    w_gate,
    w_up,
    w_down,
):
    tok_rows, model_width = residual.shape
    req_size = lax.axis_size("req")
    exp_size = lax.axis_size("exp")
    expert_count = req_size * exp_size
    top_count = routes.shape[1]
    capacity = max(2, 2 * tok_rows * top_count // expert_count)
    slot_count = expert_count * capacity
    half = model_width // 2

    attend = functools.partial(
        attention,
        cache_len,
        accepted_leaf,
        parents,
        q_gain,
        k_gain,
        q_proj,
        kv_proj,
        cache_k[0],
        cache_v[0],
    )
    left, left_keys, *made = attend(0, None)
    right, right_keys = attend(1, made)
    new_keys, new_values = append(
        cache_len, made[3], kv_proj, [left_keys, right_keys], cache_k[0], cache_v[0]
    )
    slots = slot_table(routes, expert_count, capacity)
    pick, mix = gather_plan(slots, route_gates, slot_count)

    inner = left.shape[1]
    up_left, down_left = shift(left, -1, req_size), shift(left, 1, req_size)
    up_right, down_right = shift(right, -1, req_size), shift(right, 1, req_size)
    far_left = shift(up_left, -1, req_size)
    far_right = shift(down_right, 1, req_size)

    def project(a, b):
        return (matmul(a, o_weight[:inner]) + matmul(b, o_weight[inner:])).astype(BF16)

    own = project(left, right)
    from_up = shift(project(up_left, up_right), 1, req_size)
    from_down = shift(project(down_left, down_right), -1, req_size)
    from_far = shift(project(far_left, far_right), 2, req_size)
    pieces = [own, from_down, from_far, from_up]
    at = lax.axis_index("req").astype(jnp.int32)
    columns = []
    for j in range(req_size):
        step = lax.rem(j - at + req_size, req_size)
        column = pieces[0]
        for s in range(1, req_size):
            column = jnp.where(step == s, pieces[s], column)
        columns.append(column)
    projected = jnp.concatenate(columns, axis=1).astype(F32)
    middle = (residual.astype(F32) + projected).astype(BF16)
    middle32 = middle.astype(F32)
    power = jnp.mean(middle32 * middle32, axis=-1, keepdims=True)
    normed = (middle32 * lax.rsqrt(power + NORM_EPS) * post_gain).astype(BF16)

    def swap(x):
        return lax.all_to_all(
            x.reshape(expert_count, capacity, -1),
            ("req", "exp"),
            split_axis=0,
            concat_axis=0,
            tiled=True,
        ).reshape(slot_count, -1)

    parts = (slice(0, half), slice(half, model_width))
    arrived = [swap(matmul(pick, normed[:, part]).astype(BF16)) for part in parts]
    gate = up = 0.0
    for x, part in zip(arrived, parts):
        gate = gate + matmul(x, w_gate[0, part])
        up = up + matmul(x, w_up[0, part])
    hidden = (jax.nn.silu(gate) * up).astype(BF16)
    outs = []
    for part in parts:
        back = swap(matmul(hidden, w_down[0, :, part]).astype(BF16))
        mixture = matmul(mix, back)
        outs.append(middle32[:, part] + (mixture[:tok_rows] + mixture[tok_rows:]))
    hidden_out = jnp.concatenate(outs, axis=1).astype(BF16)
    return (hidden_out, new_keys[None], new_values[None])


def solution(mesh):
    placed = (
        P(("req", "exp"), None),
        P(("req", "exp"), None),
        P(("req", "exp"), None),
        P(),
        P(),
        P(("req", "exp"), None, None),
        P(("req", "exp"), None, None),
        P(("req", "exp")),
        P(("req", "exp"), None),
        P(("req", "exp")),
        P(None, "req"),
        P(),
        P(("req", "exp"), None),
        P(("req", "exp"), None),
        P(("req", "exp"), None, None),
        P(("req", "exp"), None, None),
        P(("req", "exp"), None, None),
    )
    return jax.shard_map(
        shards,
        mesh=mesh,
        in_specs=placed,
        out_specs=(
            P(("req", "exp"), None),
            P(("req", "exp"), None, None),
            P(("req", "exp"), None, None),
        ),
        check_vma=False,
    )
```

```python
import functools

import jax
import jax.numpy as jnp
import numpy as np
from jax import lax
from jax.experimental import pallas as pl
from jax.experimental.pallas import tpu as pltpu
from jax.sharding import PartitionSpec as P


HEADS = 32
KV_HEADS = 4
WINDOW = 512
SINKS = 4

ROPE_BASE = 1000000.0
NORM_EPS = 1e-06
MASKED = -1e30

F32 = jnp.float32
BF16 = jnp.bfloat16


def matmul(a, b):
    return jnp.dot(a, b, preferred_element_type=F32)


def contract(a, b, dims_a, dims_b):
    return lax.dot_general(a, b, (((dims_a,), (dims_b,)), ((), ())), preferred_element_type=F32)


def iota(shape, axis):
    return lax.broadcasted_iota(jnp.int32, shape, axis)


def tables(length, leaf, parents_ref, freq_ref, span, slots, patch):
    draft = parents_ref.shape[1]
    width = freq_ref.shape[1]
    child = iota((draft, draft), 1)
    node = iota((draft, draft), 0)
    eye = (child == node).astype(F32)
    links = (eye + (parents_ref[...] == node).astype(F32)).astype(BF16)
    for _ in range((draft - 1).bit_length()):
        links = jnp.minimum(matmul(links, links), 1.0).astype(BF16)
    closure = contract(links, eye.astype(BF16), 0, 0)
    depth = jnp.sum(closure, axis=1, keepdims=True) - 1.0
    angle = (length.astype(F32) + depth) * freq_ref[...]
    sine = jnp.sin(angle)
    sine = jnp.where(iota((draft, width), 1) < width // 2, -sine, sine)
    head = iota((draft, width - draft), 1)
    first = jnp.minimum(jnp.maximum(length - WINDOW, 0) // 16 * 16, slots - span)
    seen = (head < SINKS) & (head < length) & (head < first)
    tree = jnp.concatenate(
        [jnp.where(closure > 0.5, 0.0, MASKED), jnp.where(seen, 0.0, MASKED)], axis=1
    )
    chosen = (iota((8, draft), 1) == leaf).astype(BF16)
    accepted = matmul(chosen, closure.astype(BF16))[:1]
    depths = contract(jnp.ones((8, draft), BF16), closure.astype(BF16), 1, 1)[:1] - 1.0
    row = iota((patch, draft), 0) + patch_start(length, slots, patch) - length
    place = ((row == depths.astype(jnp.int32)) & (accepted > 0.5)).astype(BF16)
    return jnp.cos(angle), sine, tree, place


def patch_start(length, slots, patch):
    return jnp.minimum(length // 16 * 16, slots - patch)


def attention_kernel(opening, span, *refs):
    length_ref, leaf_ref, q_gain_ref, k_gain_ref, q_ref, k_ref, v_ref, cache_k_ref, cache_v_ref = refs[:9]
    refs = refs[9:]
    if opening:
        parents_ref, freq_ref, out_ref, key_ref, cos_ref, sin_ref, tree_ref, place_ref = refs
    else:
        cos_ref, sin_ref, tree_ref, out_ref, key_ref = refs
    draft = k_ref.shape[0]
    width = k_ref.shape[1]
    slots = cache_k_ref.shape[0]
    group = q_ref.shape[1] // width
    length = length_ref[0]

    if opening:

        @pl.when(pl.program_id(0) == 0)
        def _():
            made = tables(
                length, leaf_ref[0], parents_ref, freq_ref, span, slots, place_ref.shape[0]
            )
            for ref, table in zip((cos_ref, sin_ref, tree_ref, place_ref), made):
                ref[...] = table

    cosine = cos_ref[...]
    sine = sin_ref[...]

    def turned(x, gain):
        x = x * lax.rsqrt(jnp.mean(x * x, axis=-1, keepdims=True) + NORM_EPS) * gain
        return x, pltpu.roll(x, width // 2, axis=1)

    k_new, k_swapped = turned(k_ref[...].astype(F32), k_gain_ref[...])
    k_new = (k_new * cosine + k_swapped * sine).astype(BF16)
    key_ref[...] = k_new
    queries = q_ref[...].astype(F32)
    queries = jnp.concatenate(
        [queries[:, h * width : (h + 1) * width] for h in range(group)], axis=0
    )
    queries, q_swapped = turned(queries, q_gain_ref[...])
    shape = (group, draft, width)
    queries = (
        queries.reshape(shape) * cosine[None] + q_swapped.reshape(shape) * sine[None]
    ).reshape(group * draft, width).astype(BF16)

    first = jnp.minimum(jnp.maximum(length - WINDOW, 0) // 16 * 16, slots - span)
    first = pl.multiple_of(first, 16)
    pad = jnp.zeros((width - draft - 16, width), BF16)
    keys = cache_k_ref[pl.ds(first, span), :]
    values = cache_v_ref[pl.ds(first, span), :]
    own_keys = jnp.concatenate([k_new, cache_k_ref[:16, :], pad], axis=0)
    own_values = jnp.concatenate([v_ref[...], cache_v_ref[:16, :], pad], axis=0)
    slot = iota((1, span), 1) + first
    seen = (slot < length) & ((slot < SINKS) | (slot >= length - WINDOW))
    far = contract(queries, keys, 1, 1) + jnp.where(seen, 0.0, MASKED)
    near = contract(queries, own_keys, 1, 1).reshape(shape) + tree_ref[...][None]
    near = near.reshape(group * draft, width)
    top = jnp.maximum(
        jnp.max(far, axis=-1, keepdims=True), jnp.max(near, axis=-1, keepdims=True)
    )
    scale = float(width) ** -0.5 * float(np.log2(np.e))
    far = jnp.exp2((far - top) * scale)
    near = jnp.exp2((near - top) * scale)
    total = jnp.sum(far, axis=-1, keepdims=True) + jnp.sum(near, axis=-1, keepdims=True)
    mixed = matmul(far.astype(BF16), values) + matmul(near.astype(BF16), own_values)
    mixed = (mixed / total).astype(BF16)
    for h in range(group):
        out_ref[:, h * width : (h + 1) * width] = mixed[h * draft : (h + 1) * draft]


def attention(length, leaf, parents, q_gain, k_gain, q_proj, kv_proj, cache_k, cache_v, at, made):
    draft = q_proj.shape[0]
    width = q_gain.shape[0]
    slots = cache_k.shape[0]
    span = min(slots, WINDOW + 128)
    per_group = HEADS // KV_HEADS * width
    groups = KV_HEADS // 2
    base = at * groups
    smem = pl.BlockSpec(memory_space=pltpu.SMEM)
    whole = lambda shape: pl.BlockSpec(shape, lambda g: (0, 0))
    table = jax.ShapeDtypeStruct((draft, width), F32)
    patch = draft + 16
    tables_shape = [table] * 3 + [jax.ShapeDtypeStruct((patch, draft), BF16)]
    in_specs = [
        smem,
        smem,
        whole((1, width)),
        whole((1, width)),
        pl.BlockSpec((draft, per_group), lambda g: (0, g + base)),
        pl.BlockSpec((draft, width), lambda g: (0, g + base)),
        pl.BlockSpec((draft, width), lambda g: (0, g + base + KV_HEADS)),
        pl.BlockSpec((slots, width), lambda g: (0, g + base)),
        pl.BlockSpec((slots, width), lambda g: (0, g + base)),
    ]
    out_specs = [
        pl.BlockSpec((draft, per_group), lambda g: (0, g)),
        pl.BlockSpec((draft, width), lambda g: (0, g)),
    ]
    out_shape = [
        jax.ShapeDtypeStruct((draft, per_group * groups), BF16),
        jax.ShapeDtypeStruct((draft, width * groups), BF16),
    ]
    operands = [length, leaf, q_gain[None], k_gain[None], q_proj, kv_proj, kv_proj, cache_k, cache_v]
    if made is None:
        half = width // 2
        freq = ROPE_BASE ** (-(np.arange(half) * 2.0) / width)
        freq = jnp.asarray(np.concatenate([freq, freq])[None, :], F32)
        operands += [parents, freq]
        in_specs += [whole((1, draft)), whole((1, width))]
        out_specs += [whole(t.shape) for t in tables_shape]
        out_shape += tables_shape
    else:
        operands += made[:3]
        in_specs += [whole(t.shape) for t in made[:3]]
    return pl.pallas_call(
        functools.partial(attention_kernel, made is None, span),
        grid=(groups,),
        in_specs=in_specs,
        out_specs=out_specs,
        out_shape=out_shape,
        cost_estimate=pl.CostEstimate(
            flops=2 * HEADS * draft * (span + width) * width,
            bytes_accessed=2 << 20,
            transcendentals=HEADS // 2 * draft * (span + width),
        ),
    )(*operands)


def append_kernel(length_ref, place_ref, cache_ref, *rest):
    new_ref = rest[-1]
    patch = place_ref.shape[0]
    slots = cache_ref.shape[0]
    at = pl.multiple_of(patch_start(length_ref[0], slots, patch), 16)
    place = place_ref[...]
    taken = jnp.sum(place.astype(F32), axis=1, keepdims=True) > 0.5
    rows = pl.ds(at, patch)
    fresh = rest[0][...]
    if len(rest) > 2:
        fresh = jnp.where(pl.program_id(0) == 0, fresh, rest[1][...])
    new_ref[...] = cache_ref[...]
    put = matmul(place, fresh).astype(BF16)
    new_ref[rows, :] = jnp.where(taken, put, cache_ref[rows, :])


def append(length, place, cache, fresh):
    slots, width = cache.shape
    draft = place.shape[1]
    cols = width // 2
    whole = lambda x: pl.BlockSpec(x.shape, lambda g: (0, 0))
    cache_spec = pl.BlockSpec((slots, cols), lambda g: (0, g))
    last = [pl.BlockSpec((draft, cols), lambda g: (0, g + 2))]
    return pl.pallas_call(
        append_kernel,
        grid=(2,),
        in_specs=[pl.BlockSpec(memory_space=pltpu.SMEM), whole(place), cache_spec]
        + (last if len(fresh) == 1 else [whole(x) for x in fresh]),
        out_specs=cache_spec,
        out_shape=jax.ShapeDtypeStruct(cache.shape, BF16),
        cost_estimate=pl.CostEstimate(
            flops=4 * place.shape[0] * draft * cols,
            bytes_accessed=4 * slots * width,
            transcendentals=0,
        ),
    )(length, place, cache, *fresh)


def second_kernel(x_ref, gate_ref, up_ref, down_ref, gate_in, up_in, hidden_out, sent_out):
    x = x_ref[...]
    gate = matmul(x, gate_ref[...]) + gate_in[...]
    up = matmul(x, up_ref[...]) + up_in[...]
    hidden = (gate / (1.0 + jnp.exp(-gate)) * up).astype(BF16)
    hidden_out[...] = hidden
    sent_out[...] = matmul(hidden, down_ref[...]).astype(BF16)


def second_half(x, w_gate, w_up, w_down, gate, up):
    count, cols = x.shape
    width = w_gate.shape[1]
    rows = 128
    once = pl.Buffered(1)
    by_rows = lambda n: pl.BlockSpec((rows, n), lambda i: (i, 0))
    part = pl.BlockSpec((cols, width), lambda i: (1, 0), pipeline_mode=once)
    down = pl.BlockSpec((width, cols), lambda i: (0, 0), pipeline_mode=once)
    return pl.pallas_call(
        second_kernel,
        grid=(count // rows,),
        in_specs=[by_rows(cols), part, part, down, by_rows(width), by_rows(width)],
        out_specs=[by_rows(width), by_rows(cols)],
        out_shape=[
            jax.ShapeDtypeStruct((count, width), BF16),
            jax.ShapeDtypeStruct((count, cols), BF16),
        ],
        name="experts_second",
        cost_estimate=pl.CostEstimate(
            flops=6 * count * cols * width, bytes_accessed=16 << 20, transcendentals=count * width
        ),
    )(x, w_gate, w_up, w_down, gate, up)


def down_kernel(hidden_ref, down_ref, out_ref):
    out_ref[...] = matmul(hidden_ref[...], down_ref[...]).astype(BF16)


def last_columns(hidden, w_down, cols):
    count, width = hidden.shape
    rows = 256
    return pl.pallas_call(
        down_kernel,
        grid=(count // rows,),
        in_specs=[
            pl.BlockSpec((rows, width), lambda i: (i, 0)),
            pl.BlockSpec((width, cols), lambda i: (0, 1), pipeline_mode=pl.Buffered(1)),
        ],
        out_specs=pl.BlockSpec((rows, cols), lambda i: (i, 0)),
        out_shape=jax.ShapeDtypeStruct((count, cols), BF16),
        name="experts_third",
        cost_estimate=pl.CostEstimate(
            flops=2 * count * cols * width, bytes_accessed=5 << 20, transcendentals=0
        ),
    )(hidden, w_down)


def slot_table(routes, expert_count, capacity):
    tokens = routes.shape[0]
    onehot = routes[:, :, None] == jnp.arange(expert_count, dtype=jnp.int32)[None, None, :]
    used = jnp.any(onehot, axis=1).astype(BF16)
    earlier = jnp.asarray(np.tril(np.ones((tokens, tokens)), -1), BF16)
    rank = matmul(earlier, used)
    rank = jnp.sum(jnp.where(onehot, rank[:, None, :], 0.0), axis=2).astype(jnp.int32)
    return routes * capacity + rank


def gather_plan(slots, gates, slot_count):
    index = jnp.arange(slot_count, dtype=jnp.int32)
    slots_t = slots.T
    pick = index[:, None] == slots_t[0][None, :]
    mix = jnp.where(index[None, :] == slots[:, :1], gates[:, :1], 0.0)
    for k in range(1, slots.shape[1]):
        pick = pick | (index[:, None] == slots_t[k][None, :])
        mix = jnp.where(index[None, :] == slots[:, k : k + 1], gates[:, k : k + 1], mix)
    high = lax.reduce_precision(mix, 8, 7)
    return pick.astype(BF16), jnp.concatenate([high, mix - high], axis=0).astype(BF16)


def shift(x, by, size):
    return lax.ppermute(x, "req", [(i, (i + by) % size) for i in range(size)])


def body(
    residual,
    q_proj,
    kv_proj,
    q_gain,
    k_gain,
    cache_k,
    cache_v,
    cache_len,
    parents,
    accepted_leaf,
    o_weight,
    post_gain,
    routes,
    route_gates,
    w_gate,
    w_up,
    w_down,
):
    tok_rows, model_width = residual.shape
    req_size = lax.axis_size("req")
    exp_size = lax.axis_size("exp")
    expert_count = req_size * exp_size
    top_count = routes.shape[1]
    capacity = max(2, 2 * tok_rows * top_count // expert_count)
    slot_count = expert_count * capacity
    half = model_width // 2

    attend = functools.partial(
        attention,
        cache_len,
        accepted_leaf,
        parents,
        q_gain,
        k_gain,
        q_proj,
        kv_proj,
        cache_k[0],
        cache_v[0],
    )
    left, left_keys, *made = attend(0, None)
    right, right_keys = attend(1, made)
    new_keys = append(cache_len, made[3], cache_k[0], [left_keys, right_keys])
    new_values = append(cache_len, made[3], cache_v[0], [kv_proj])
    slots = slot_table(routes, expert_count, capacity)
    pick, mix = gather_plan(slots, route_gates, slot_count)

    inner = left.shape[1]
    up_left, down_left = shift(left, -1, req_size), shift(left, 1, req_size)
    up_right, down_right = shift(right, -1, req_size), shift(right, 1, req_size)
    far_left = shift(up_left, -1, req_size)
    far_right = shift(down_right, 1, req_size)

    def project(a, b):
        return (matmul(a, o_weight[:inner]) + matmul(b, o_weight[inner:])).astype(BF16)

    own = project(left, right)
    near_up = project(up_left, up_right)
    near_down = project(down_left, down_right)
    from_up = shift(near_up, 1, req_size)
    from_down = shift(near_down, -1, req_size)
    from_far = shift(project(far_left, far_right), 2, req_size)
    pieces = [own, from_down, from_far, from_up]
    at = lax.axis_index("req").astype(jnp.int32)
    columns = []
    for j in range(req_size):
        step = lax.rem(j - at + req_size, req_size)
        column = pieces[0]
        for s in range(1, req_size):
            column = jnp.where(step == s, pieces[s], column)
        columns.append(column)
    projected = jnp.concatenate(columns, axis=1).astype(F32)
    middle = (residual.astype(F32) + projected).astype(BF16)
    middle32 = middle.astype(F32)
    power = jnp.mean(middle32 * middle32, axis=-1, keepdims=True)
    normed = (middle32 * lax.rsqrt(power + NORM_EPS) * post_gain).astype(BF16)

    def swap(x):
        return lax.all_to_all(
            x.reshape(expert_count, capacity, -1),
            ("req", "exp"),
            split_axis=0,
            concat_axis=0,
            tiled=True,
        ).reshape(slot_count, -1)

    parts = (slice(0, half), slice(half, model_width))
    arrived = [swap(matmul(pick, normed[:, part]).astype(BF16)) for part in parts]
    gate = matmul(arrived[0], w_gate[0, parts[0]])
    up = matmul(arrived[0], w_up[0, parts[0]])
    hidden, sent = second_half(arrived[1], w_gate[0], w_up[0], w_down[0], gate, up)
    sent = [sent, last_columns(hidden, w_down[0], half)]
    outs = []
    for part, out in zip(parts, sent):
        mixture = matmul(mix, swap(out))
        outs.append(middle32[:, part] + (mixture[:tok_rows] + mixture[tok_rows:]))
    hidden_out = jnp.concatenate(outs, axis=1).astype(BF16)
    return (hidden_out, new_keys[None], new_values[None])


def solution(mesh):
    placed = (
        P(("req", "exp"), None),
        P(("req", "exp"), None),
        P(("req", "exp"), None),
        P(),
        P(),
        P(("req", "exp"), None, None),
        P(("req", "exp"), None, None),
        P(("req", "exp")),
        P(("req", "exp"), None),
        P(("req", "exp")),
        P(None, "req"),
        P(),
        P(("req", "exp"), None),
        P(("req", "exp"), None),
        P(("req", "exp"), None, None),
        P(("req", "exp"), None, None),
        P(("req", "exp"), None, None),
    )
    return jax.shard_map(
        body,
        mesh=mesh,
        in_specs=placed,
        out_specs=(
            P(("req", "exp"), None),
            P(("req", "exp"), None, None),
            P(("req", "exp"), None, None),
        ),
        check_vma=False,
    )
```

```python
import functools

import jax
import jax.numpy as jnp
import numpy as np
from jax import lax
from jax.experimental import pallas as pl
from jax.experimental.pallas import tpu as pltpu
from jax.sharding import PartitionSpec as P


HEADS = 32
KV_HEADS = 4
WINDOW = 512
SINKS = 4

ROPE_BASE = 1000000.0
NORM_EPS = 1e-06
MASKED = -1e30

F32 = jnp.float32
BF16 = jnp.bfloat16


def matmul(a, b):
    return jnp.dot(a, b, preferred_element_type=F32)


def contract(a, b, dims_a, dims_b):
    return lax.dot_general(a, b, (((dims_a,), (dims_b,)), ((), ())), preferred_element_type=F32)


def iota(shape, axis):
    return lax.broadcasted_iota(jnp.int32, shape, axis)


def tables(length, leaf, parents_ref, freq_ref, span, slots, patch):
    draft = parents_ref.shape[1]
    width = freq_ref.shape[1]
    child = iota((draft, draft), 1)
    node = iota((draft, draft), 0)
    eye = (child == node).astype(F32)
    links = (eye + (parents_ref[...] == node).astype(F32)).astype(BF16)
    for _ in range((draft - 1).bit_length()):
        links = jnp.minimum(matmul(links, links), 1.0).astype(BF16)
    closure = contract(links, eye.astype(BF16), 0, 0)
    depth = jnp.sum(closure, axis=1, keepdims=True) - 1.0
    angle = (length.astype(F32) + depth) * freq_ref[...]
    sine = jnp.sin(angle)
    sine = jnp.where(iota((draft, width), 1) < width // 2, -sine, sine)
    head = iota((draft, width - draft), 1)
    first = jnp.minimum(jnp.maximum(length - WINDOW, 0) // 16 * 16, slots - span)
    seen = (head < SINKS) & (head < length) & (head < first)
    tree = jnp.concatenate(
        [jnp.where(closure > 0.5, 0.0, MASKED), jnp.where(seen, 0.0, MASKED)], axis=1
    )
    chosen = (iota((8, draft), 1) == leaf).astype(BF16)
    accepted = matmul(chosen, closure.astype(BF16))[:1]
    depths = contract(jnp.ones((8, draft), BF16), closure.astype(BF16), 1, 1)[:1] - 1.0
    row = iota((patch, draft), 0) + patch_start(length, slots, patch) - length
    place = ((row == depths.astype(jnp.int32)) & (accepted > 0.5)).astype(BF16)
    return jnp.cos(angle), sine, tree, place


def patch_start(length, slots, patch):
    return jnp.minimum(length // 16 * 16, slots - patch)


def attention_kernel(opening, span, *refs):
    length_ref, leaf_ref, q_gain_ref, k_gain_ref, q_ref, k_ref, v_ref, cache_k_ref, cache_v_ref = refs[:9]
    refs = refs[9:]
    if opening:
        parents_ref, freq_ref, out_ref, key_ref, cos_ref, sin_ref, tree_ref, place_ref = refs
    else:
        cos_ref, sin_ref, tree_ref, out_ref, key_ref = refs
    draft = k_ref.shape[0]
    width = k_ref.shape[1]
    slots = cache_k_ref.shape[0]
    group = q_ref.shape[1] // width
    length = length_ref[0]

    if opening:

        @pl.when(pl.program_id(0) == 0)
        def _():
            made = tables(
                length, leaf_ref[0], parents_ref, freq_ref, span, slots, place_ref.shape[0]
            )
            for ref, table in zip((cos_ref, sin_ref, tree_ref, place_ref), made):
                ref[...] = table

    cosine = cos_ref[...]
    sine = sin_ref[...]

    def turned(x, gain):
        x = x * lax.rsqrt(jnp.mean(x * x, axis=-1, keepdims=True) + NORM_EPS) * gain
        return x, pltpu.roll(x, width // 2, axis=1)

    k_new, k_swapped = turned(k_ref[...].astype(F32), k_gain_ref[...])
    k_new = (k_new * cosine + k_swapped * sine).astype(BF16)
    key_ref[...] = k_new
    queries = q_ref[...].astype(F32)
    queries = jnp.concatenate(
        [queries[:, h * width : (h + 1) * width] for h in range(group)], axis=0
    )
    queries, q_swapped = turned(queries, q_gain_ref[...])
    shape = (group, draft, width)
    queries = (
        queries.reshape(shape) * cosine[None] + q_swapped.reshape(shape) * sine[None]
    ).reshape(group * draft, width).astype(BF16)

    first = jnp.minimum(jnp.maximum(length - WINDOW, 0) // 16 * 16, slots - span)
    first = pl.multiple_of(first, 16)
    pad = jnp.zeros((width - draft - 16, width), BF16)
    keys = cache_k_ref[pl.ds(first, span), :]
    values = cache_v_ref[pl.ds(first, span), :]
    own_keys = jnp.concatenate([k_new, cache_k_ref[:16, :], pad], axis=0)
    own_values = jnp.concatenate([v_ref[...], cache_v_ref[:16, :], pad], axis=0)
    slot = iota((1, span), 1) + first
    seen = (slot < length) & ((slot < SINKS) | (slot >= length - WINDOW))
    far = contract(queries, keys, 1, 1) + jnp.where(seen, 0.0, MASKED)
    near = contract(queries, own_keys, 1, 1).reshape(shape) + tree_ref[...][None]
    near = near.reshape(group * draft, width)
    top = jnp.maximum(
        jnp.max(far, axis=-1, keepdims=True), jnp.max(near, axis=-1, keepdims=True)
    )
    scale = float(width) ** -0.5 * float(np.log2(np.e))
    far = jnp.exp2((far - top) * scale)
    near = jnp.exp2((near - top) * scale)
    total = jnp.sum(far, axis=-1, keepdims=True) + jnp.sum(near, axis=-1, keepdims=True)
    mixed = matmul(far.astype(BF16), values) + matmul(near.astype(BF16), own_values)
    mixed = (mixed / total).astype(BF16)
    for h in range(group):
        out_ref[:, h * width : (h + 1) * width] = mixed[h * draft : (h + 1) * draft]


def attention(length, leaf, parents, q_gain, k_gain, q_proj, kv_proj, cache_k, cache_v, at, made):
    draft = q_proj.shape[0]
    width = q_gain.shape[0]
    slots = cache_k.shape[0]
    span = min(slots, WINDOW + 128)
    per_group = HEADS // KV_HEADS * width
    groups = KV_HEADS // 2
    base = at * groups
    smem = pl.BlockSpec(memory_space=pltpu.SMEM)
    whole = lambda shape: pl.BlockSpec(shape, lambda g: (0, 0))
    table = jax.ShapeDtypeStruct((draft, width), F32)
    patch = draft + 16
    tables_shape = [table] * 3 + [jax.ShapeDtypeStruct((patch, draft), BF16)]
    in_specs = [
        smem,
        smem,
        whole((1, width)),
        whole((1, width)),
        pl.BlockSpec((draft, per_group), lambda g: (0, g + base)),
        pl.BlockSpec((draft, width), lambda g: (0, g + base)),
        pl.BlockSpec((draft, width), lambda g: (0, g + base + KV_HEADS)),
        pl.BlockSpec((slots, width), lambda g: (0, g + base)),
        pl.BlockSpec((slots, width), lambda g: (0, g + base)),
    ]
    out_specs = [
        pl.BlockSpec((draft, per_group), lambda g: (0, g)),
        pl.BlockSpec((draft, width), lambda g: (0, g)),
    ]
    out_shape = [
        jax.ShapeDtypeStruct((draft, per_group * groups), BF16),
        jax.ShapeDtypeStruct((draft, width * groups), BF16),
    ]
    operands = [length, leaf, q_gain[None], k_gain[None], q_proj, kv_proj, kv_proj, cache_k, cache_v]
    if made is None:
        half = width // 2
        freq = ROPE_BASE ** (-(np.arange(half) * 2.0) / width)
        freq = jnp.asarray(np.concatenate([freq, freq])[None, :], F32)
        operands += [parents, freq]
        in_specs += [whole((1, draft)), whole((1, width))]
        out_specs += [whole(t.shape) for t in tables_shape]
        out_shape += tables_shape
    else:
        operands += made[:3]
        in_specs += [whole(t.shape) for t in made[:3]]
    return pl.pallas_call(
        functools.partial(attention_kernel, made is None, span),
        grid=(groups,),
        in_specs=in_specs,
        out_specs=out_specs,
        out_shape=out_shape,
        cost_estimate=pl.CostEstimate(
            flops=2 * HEADS * draft * (span + width) * width,
            bytes_accessed=2 << 20,
            transcendentals=HEADS // 2 * draft * (span + width),
        ),
    )(*operands)


def append_kernel(length_ref, place_ref, cache_ref, *rest):
    new_ref = rest[-1]
    patch = place_ref.shape[0]
    slots = cache_ref.shape[0]
    at = pl.multiple_of(patch_start(length_ref[0], slots, patch), 16)
    place = place_ref[...]
    taken = jnp.sum(place.astype(F32), axis=1, keepdims=True) > 0.5
    rows = pl.ds(at, patch)
    fresh = rest[0][...]
    if len(rest) > 2:
        fresh = jnp.where(pl.program_id(0) == 0, fresh, rest[1][...])
    new_ref[...] = cache_ref[...]
    put = matmul(place, fresh).astype(BF16)
    new_ref[rows, :] = jnp.where(taken, put, cache_ref[rows, :])


def append(length, place, cache, fresh):
    slots, width = cache.shape
    draft = place.shape[1]
    cols = width // 2
    whole = lambda x: pl.BlockSpec(x.shape, lambda g: (0, 0))
    cache_spec = pl.BlockSpec((slots, cols), lambda g: (0, g))
    last = [pl.BlockSpec((draft, cols), lambda g: (0, g + 2))]
    return pl.pallas_call(
        append_kernel,
        grid=(2,),
        in_specs=[pl.BlockSpec(memory_space=pltpu.SMEM), whole(place), cache_spec]
        + (last if len(fresh) == 1 else [whole(x) for x in fresh]),
        out_specs=cache_spec,
        out_shape=jax.ShapeDtypeStruct(cache.shape, BF16),
        cost_estimate=pl.CostEstimate(
            flops=4 * place.shape[0] * draft * cols,
            bytes_accessed=4 * slots * width,
            transcendentals=0,
        ),
    )(length, place, cache, *fresh)


def outbox_kernel(pick_ref, middle_ref, gain_ref, out_ref, normed_ref):
    @pl.when(pl.program_id(0) == 0)
    def _():
        middle = middle_ref[...].astype(F32)
        power = jnp.mean(middle * middle, axis=-1, keepdims=True)
        normed_ref[...] = (middle * lax.rsqrt(power + NORM_EPS) * gain_ref[...]).astype(BF16)

    out_ref[...] = matmul(pick_ref[...], normed_ref[...]).astype(BF16)


def outbox(pick, middle, gain):
    count, tokens = pick.shape
    width = middle.shape[1]
    rows = 256
    return pl.pallas_call(
        outbox_kernel,
        grid=(count // rows,),
        in_specs=[
            pl.BlockSpec((rows, tokens), lambda i: (i, 0)),
            pl.BlockSpec((tokens, width), lambda i: (0, 0)),
            pl.BlockSpec((1, width), lambda i: (0, 0)),
        ],
        out_specs=pl.BlockSpec((rows, width), lambda i: (i, 0)),
        out_shape=jax.ShapeDtypeStruct((count, width), BF16),
        scratch_shapes=[pltpu.VMEM((tokens, width), BF16)],
        name="outbox",
        cost_estimate=pl.CostEstimate(
            flops=2 * count * tokens * width, bytes_accessed=2 * count * width, transcendentals=0
        ),
    )(pick, middle, gain)


INNER = 3
OUTER = 2


def experts_kernel(x_ref, gate_ref, up_ref, down_ref, out_ref, hidden_ref):
    step = pl.program_id(1)

    @pl.when(step < INNER)
    def _():
        x = x_ref[...]
        gate = matmul(x, gate_ref[...])
        up = matmul(x, up_ref[...])
        hidden_ref[step] = (gate / (1.0 + jnp.exp(-gate)) * up).astype(BF16)

    @pl.when(step >= INNER)
    def _():
        hidden = jnp.concatenate([hidden_ref[j] for j in range(INNER)], axis=1)
        out_ref[...] = matmul(hidden, down_ref[...]).astype(BF16)


def experts(x, w_gate, w_up, w_down):
    count, width = x.shape
    inner = w_gate.shape[1]
    rows = count // 2
    cut = inner // INNER
    cols = width // OUTER
    entry = pl.BlockSpec((width, cut), lambda i, j: (0, jnp.where(j < INNER, j, 0)))
    leave = lambda j: jnp.maximum(j - INNER, 0)
    return pl.pallas_call(
        experts_kernel,
        grid=(2, INNER + OUTER),
        in_specs=[
            pl.BlockSpec((rows, width), lambda i, j: (i, 0)),
            entry,
            entry,
            pl.BlockSpec((inner, cols), lambda i, j: (0, leave(j))),
        ],
        out_specs=pl.BlockSpec((rows, cols), lambda i, j: (i, leave(j))),
        out_shape=jax.ShapeDtypeStruct((count, width), BF16),
        scratch_shapes=[pltpu.VMEM((INNER, rows, cut), BF16)],
        name="experts",
        cost_estimate=pl.CostEstimate(
            flops=6 * count * width * inner,
            bytes_accessed=4 * count * width + 12 * width * inner,
            transcendentals=count * inner,
        ),
    )(x, w_gate, w_up, w_down)


def combine_kernel(mix_ref, middle_ref, returned_ref, out_ref):
    mixture = matmul(mix_ref[...], returned_ref[...])
    tokens = middle_ref.shape[0]
    mixture = mixture[:tokens] + mixture[tokens:]
    out_ref[...] = (middle_ref[...].astype(F32) + mixture).astype(BF16)


def combine(mix, middle, returned):
    count, width = returned.shape
    tokens = middle.shape[0]
    cols = width // 4
    return pl.pallas_call(
        combine_kernel,
        grid=(4,),
        in_specs=[
            pl.BlockSpec(mix.shape, lambda i: (0, 0)),
            pl.BlockSpec((tokens, cols), lambda i: (0, i)),
            pl.BlockSpec((count, cols), lambda i: (0, i)),
        ],
        out_specs=pl.BlockSpec((tokens, cols), lambda i: (0, i)),
        out_shape=jax.ShapeDtypeStruct(middle.shape, BF16),
        name="combine",
        cost_estimate=pl.CostEstimate(
            flops=4 * tokens * count * width, bytes_accessed=2 * count * width, transcendentals=0
        ),
    )(mix, middle, returned)


def slot_table(routes, expert_count, capacity):
    tokens = routes.shape[0]
    onehot = routes[:, :, None] == jnp.arange(expert_count, dtype=jnp.int32)[None, None, :]
    used = jnp.any(onehot, axis=1).astype(BF16)
    earlier = jnp.asarray(np.tril(np.ones((tokens, tokens)), -1), BF16)
    rank = matmul(earlier, used)
    rank = jnp.sum(jnp.where(onehot, rank[:, None, :], 0.0), axis=2).astype(jnp.int32)
    return routes * capacity + rank


def gather_plan(slots, gates, slot_count):
    index = jnp.arange(slot_count, dtype=jnp.int32)
    slots_t = slots.T
    pick = index[:, None] == slots_t[0][None, :]
    mix = jnp.where(index[None, :] == slots[:, :1], gates[:, :1], 0.0)
    for k in range(1, slots.shape[1]):
        pick = pick | (index[:, None] == slots_t[k][None, :])
        mix = jnp.where(index[None, :] == slots[:, k : k + 1], gates[:, k : k + 1], mix)
    high = lax.reduce_precision(mix, 8, 7)
    return pick.astype(BF16), jnp.concatenate([high, mix - high], axis=0).astype(BF16)


def shift(x, by, size):
    return lax.ppermute(x, "req", [(i, (i + by) % size) for i in range(size)])


def body(
    residual,
    q_proj,
    kv_proj,
    q_gain,
    k_gain,
    cache_k,
    cache_v,
    cache_len,
    parents,
    accepted_leaf,
    o_weight,
    post_gain,
    routes,
    route_gates,
    w_gate,
    w_up,
    w_down,
):
    tok_rows, model_width = residual.shape
    req_size = lax.axis_size("req")
    exp_size = lax.axis_size("exp")
    expert_count = req_size * exp_size
    top_count = routes.shape[1]
    capacity = max(2, 2 * tok_rows * top_count // expert_count)
    slot_count = expert_count * capacity

    attend = functools.partial(
        attention,
        cache_len,
        accepted_leaf,
        parents,
        q_gain,
        k_gain,
        q_proj,
        kv_proj,
        cache_k[0],
        cache_v[0],
    )
    left, left_keys, *made = attend(0, None)
    right, right_keys = attend(1, made)
    new_keys = append(cache_len, made[3], cache_k[0], [left_keys, right_keys])
    new_values = append(cache_len, made[3], cache_v[0], [kv_proj])
    slots = slot_table(routes, expert_count, capacity)
    pick, mix = gather_plan(slots, route_gates, slot_count)

    inner = left.shape[1]
    up_left, down_left = shift(left, -1, req_size), shift(left, 1, req_size)
    up_right, down_right = shift(right, -1, req_size), shift(right, 1, req_size)
    far_left = shift(up_left, -1, req_size)
    far_right = shift(down_right, 1, req_size)

    def project(a, b):
        return (matmul(a, o_weight[:inner]) + matmul(b, o_weight[inner:])).astype(BF16)

    own = project(left, right)
    near_up = project(up_left, up_right)
    near_down = project(down_left, down_right)
    from_up = shift(near_up, 1, req_size)
    from_down = shift(near_down, -1, req_size)
    from_far = shift(project(far_left, far_right), 2, req_size)
    pieces = [own, from_down, from_far, from_up]
    at = lax.axis_index("req").astype(jnp.int32)
    columns = []
    for j in range(req_size):
        step = lax.rem(j - at + req_size, req_size)
        column = pieces[0]
        for s in range(1, req_size):
            column = jnp.where(step == s, pieces[s], column)
        columns.append(column)
    projected = jnp.concatenate(columns, axis=1).astype(F32)
    middle = (residual.astype(F32) + projected).astype(BF16)

    def swap(x):
        return lax.all_to_all(
            x.reshape(expert_count, capacity, model_width),
            ("req", "exp"),
            split_axis=0,
            concat_axis=0,
            tiled=True,
        ).reshape(slot_count, model_width)

    arrived = swap(outbox(pick, middle, post_gain[None]))
    returned = swap(experts(arrived, w_gate[0], w_up[0], w_down[0]))
    hidden_out = combine(mix, middle, returned)
    return (hidden_out, new_keys[None], new_values[None])


def solution(mesh):
    placed = (
        P(("req", "exp"), None),
        P(("req", "exp"), None),
        P(("req", "exp"), None),
        P(),
        P(),
        P(("req", "exp"), None, None),
        P(("req", "exp"), None, None),
        P(("req", "exp")),
        P(("req", "exp"), None),
        P(("req", "exp")),
        P(None, "req"),
        P(),
        P(("req", "exp"), None),
        P(("req", "exp"), None),
        P(("req", "exp"), None, None),
        P(("req", "exp"), None, None),
        P(("req", "exp"), None, None),
    )
    return jax.shard_map(
        body,
        mesh=mesh,
        in_specs=placed,
        out_specs=(
            P(("req", "exp"), None),
            P(("req", "exp"), None, None),
            P(("req", "exp"), None, None),
        ),
        check_vma=False,
    )
```

```python
import functools

import jax
import jax.numpy as jnp
import numpy as np
from jax import lax
from jax.experimental import pallas as pl
from jax.experimental.pallas import tpu as pltpu
from jax.sharding import PartitionSpec as P


HEADS = 32
KV_HEADS = 4
WINDOW = 512
SINKS = 4

ROPE_BASE = 1000000.0
NORM_EPS = 1e-06
MASKED = -1e30

F32 = jnp.float32
BF16 = jnp.bfloat16


def matmul(a, b):
    return jnp.dot(a, b, preferred_element_type=F32)


def contract(a, b, dims_a, dims_b):
    return lax.dot_general(a, b, (((dims_a,), (dims_b,)), ((), ())), preferred_element_type=F32)


def iota(shape, axis):
    return lax.broadcasted_iota(jnp.int32, shape, axis)


def tables(length, leaf, parents_ref, freq_ref, span, slots, patch):
    draft = parents_ref.shape[1]
    width = freq_ref.shape[1]
    child = iota((draft, draft), 1)
    node = iota((draft, draft), 0)
    eye = (child == node).astype(F32)
    links = (eye + (parents_ref[...] == node).astype(F32)).astype(BF16)
    for _ in range((draft - 1).bit_length()):
        links = jnp.minimum(matmul(links, links), 1.0).astype(BF16)
    closure = contract(links, eye.astype(BF16), 0, 0)
    depth = jnp.sum(closure, axis=1, keepdims=True) - 1.0
    angle = (length.astype(F32) + depth) * freq_ref[...]
    sine = jnp.sin(angle)
    sine = jnp.where(iota((draft, width), 1) < width // 2, -sine, sine)
    head = iota((draft, width - draft), 1)
    first = jnp.minimum(jnp.maximum(length - WINDOW, 0) // 16 * 16, slots - span)
    seen = (head < SINKS) & (head < length) & (head < first)
    tree = jnp.concatenate(
        [jnp.where(closure > 0.5, 0.0, MASKED), jnp.where(seen, 0.0, MASKED)], axis=1
    )
    chosen = (iota((8, draft), 1) == leaf).astype(BF16)
    accepted = matmul(chosen, closure.astype(BF16))[:1]
    depths = contract(jnp.ones((8, draft), BF16), closure.astype(BF16), 1, 1)[:1] - 1.0
    row = iota((patch, draft), 0) + patch_start(length, slots, patch) - length
    place = ((row == depths.astype(jnp.int32)) & (accepted > 0.5)).astype(BF16)
    return jnp.cos(angle), sine, tree, place


def patch_start(length, slots, patch):
    return jnp.minimum(length // 16 * 16, slots - patch)


def attention_kernel(opening, span, *refs):
    length_ref, leaf_ref, q_gain_ref, k_gain_ref, q_ref, k_ref, v_ref, cache_k_ref, cache_v_ref = refs[:9]
    refs = refs[9:]
    if opening:
        parents_ref, freq_ref, out_ref, key_ref, cos_ref, sin_ref, tree_ref, place_ref = refs
    else:
        cos_ref, sin_ref, tree_ref, out_ref, key_ref = refs
    draft = k_ref.shape[0]
    width = k_ref.shape[1]
    slots = cache_k_ref.shape[0]
    group = q_ref.shape[1] // width
    length = length_ref[0]

    if opening:

        @pl.when(pl.program_id(0) == 0)
        def _():
            made = tables(
                length, leaf_ref[0], parents_ref, freq_ref, span, slots, place_ref.shape[0]
            )
            for ref, table in zip((cos_ref, sin_ref, tree_ref, place_ref), made):
                ref[...] = table

    cosine = cos_ref[...]
    sine = sin_ref[...]

    def turned(x, gain):
        x = x * lax.rsqrt(jnp.mean(x * x, axis=-1, keepdims=True) + NORM_EPS) * gain
        return x, pltpu.roll(x, width // 2, axis=1)

    k_new, k_swapped = turned(k_ref[...].astype(F32), k_gain_ref[...])
    k_new = (k_new * cosine + k_swapped * sine).astype(BF16)
    key_ref[...] = k_new
    queries = q_ref[...].astype(F32)
    queries = jnp.concatenate(
        [queries[:, h * width : (h + 1) * width] for h in range(group)], axis=0
    )
    queries, q_swapped = turned(queries, q_gain_ref[...])
    shape = (group, draft, width)
    queries = (
        queries.reshape(shape) * cosine[None] + q_swapped.reshape(shape) * sine[None]
    ).reshape(group * draft, width).astype(BF16)

    first = jnp.minimum(jnp.maximum(length - WINDOW, 0) // 16 * 16, slots - span)
    first = pl.multiple_of(first, 16)
    pad = jnp.zeros((width - draft - 16, width), BF16)
    keys = cache_k_ref[pl.ds(first, span), :]
    values = cache_v_ref[pl.ds(first, span), :]
    own_keys = jnp.concatenate([k_new, cache_k_ref[:16, :], pad], axis=0)
    own_values = jnp.concatenate([v_ref[...], cache_v_ref[:16, :], pad], axis=0)
    slot = iota((1, span), 1) + first
    seen = (slot < length) & ((slot < SINKS) | (slot >= length - WINDOW))
    far = contract(queries, keys, 1, 1) + jnp.where(seen, 0.0, MASKED)
    near = contract(queries, own_keys, 1, 1).reshape(shape) + tree_ref[...][None]
    near = near.reshape(group * draft, width)
    top = jnp.maximum(
        jnp.max(far, axis=-1, keepdims=True), jnp.max(near, axis=-1, keepdims=True)
    )
    scale = float(width) ** -0.5 * float(np.log2(np.e))
    far = jnp.exp2((far - top) * scale)
    near = jnp.exp2((near - top) * scale)
    total = jnp.sum(far, axis=-1, keepdims=True) + jnp.sum(near, axis=-1, keepdims=True)
    mixed = matmul(far.astype(BF16), values) + matmul(near.astype(BF16), own_values)
    mixed = (mixed / total).astype(BF16)
    for h in range(group):
        out_ref[:, h * width : (h + 1) * width] = mixed[h * draft : (h + 1) * draft]


def attention(length, leaf, parents, q_gain, k_gain, q_proj, kv_proj, cache_k, cache_v, at, made):
    draft = q_proj.shape[0]
    width = q_gain.shape[0]
    slots = cache_k.shape[0]
    span = min(slots, WINDOW + 128)
    per_group = HEADS // KV_HEADS * width
    groups = KV_HEADS // 2
    base = at * groups
    smem = pl.BlockSpec(memory_space=pltpu.SMEM)
    whole = lambda shape: pl.BlockSpec(shape, lambda g: (0, 0))
    table = jax.ShapeDtypeStruct((draft, width), F32)
    patch = draft + 16
    tables_shape = [table] * 3 + [jax.ShapeDtypeStruct((patch, draft), BF16)]
    in_specs = [
        smem,
        smem,
        whole((1, width)),
        whole((1, width)),
        pl.BlockSpec((draft, per_group), lambda g: (0, g + base)),
        pl.BlockSpec((draft, width), lambda g: (0, g + base)),
        pl.BlockSpec((draft, width), lambda g: (0, g + base + KV_HEADS)),
        pl.BlockSpec((slots, width), lambda g: (0, g + base)),
        pl.BlockSpec((slots, width), lambda g: (0, g + base)),
    ]
    out_specs = [
        pl.BlockSpec((draft, per_group), lambda g: (0, g)),
        pl.BlockSpec((draft, width), lambda g: (0, g)),
    ]
    out_shape = [
        jax.ShapeDtypeStruct((draft, per_group * groups), BF16),
        jax.ShapeDtypeStruct((draft, width * groups), BF16),
    ]
    operands = [length, leaf, q_gain[None], k_gain[None], q_proj, kv_proj, kv_proj, cache_k, cache_v]
    if made is None:
        half = width // 2
        freq = ROPE_BASE ** (-(np.arange(half) * 2.0) / width)
        freq = jnp.asarray(np.concatenate([freq, freq])[None, :], F32)
        operands += [parents, freq]
        in_specs += [whole((1, draft)), whole((1, width))]
        out_specs += [whole(t.shape) for t in tables_shape]
        out_shape += tables_shape
    else:
        operands += made[:3]
        in_specs += [whole(t.shape) for t in made[:3]]
    return pl.pallas_call(
        functools.partial(attention_kernel, made is None, span),
        grid=(groups,),
        in_specs=in_specs,
        out_specs=out_specs,
        out_shape=out_shape,
        cost_estimate=pl.CostEstimate(
            flops=2 * HEADS * draft * (span + width) * width,
            bytes_accessed=2 << 20,
            transcendentals=HEADS // 2 * draft * (span + width),
        ),
    )(*operands)


def append_kernel(length_ref, place_ref, cache_ref, *rest):
    new_ref = rest[-1]
    patch = place_ref.shape[0]
    slots = cache_ref.shape[0]
    at = pl.multiple_of(patch_start(length_ref[0], slots, patch), 16)
    place = place_ref[...]
    taken = jnp.sum(place.astype(F32), axis=1, keepdims=True) > 0.5
    rows = pl.ds(at, patch)
    fresh = rest[0][...]
    if len(rest) > 2:
        fresh = jnp.where(pl.program_id(0) == 0, fresh, rest[1][...])
    new_ref[...] = cache_ref[...]
    put = matmul(place, fresh).astype(BF16)
    new_ref[rows, :] = jnp.where(taken, put, cache_ref[rows, :])


def append(length, place, cache, fresh):
    slots, width = cache.shape
    draft = place.shape[1]
    cols = width // 2
    whole = lambda x: pl.BlockSpec(x.shape, lambda g: (0, 0))
    cache_spec = pl.BlockSpec((slots, cols), lambda g: (0, g))
    last = [pl.BlockSpec((draft, cols), lambda g: (0, g + 2))]
    return pl.pallas_call(
        append_kernel,
        grid=(2,),
        in_specs=[pl.BlockSpec(memory_space=pltpu.SMEM), whole(place), cache_spec]
        + (last if len(fresh) == 1 else [whole(x) for x in fresh]),
        out_specs=cache_spec,
        out_shape=jax.ShapeDtypeStruct(cache.shape, BF16),
        cost_estimate=pl.CostEstimate(
            flops=4 * place.shape[0] * draft * cols,
            bytes_accessed=4 * slots * width,
            transcendentals=0,
        ),
    )(length, place, cache, *fresh)


def blocks(total, count):
    return [pl.ds(i * (total // count), total // count) for i in range(count)]


def outbox_kernel(count, pick_ref, middle_ref, gain_ref, out_hbm, normed_ref, out_buf, sems):
    middle = middle_ref[...].astype(F32)
    power = jnp.mean(middle * middle, axis=-1, keepdims=True)
    normed_ref[...] = (middle * lax.rsqrt(power + NORM_EPS) * gain_ref[...]).astype(BF16)
    copies = []
    for i, rows in enumerate(blocks(out_buf.shape[0], count)):
        out_buf[rows, :] = matmul(pick_ref[rows, :], normed_ref[...]).astype(BF16)
        copy = pltpu.make_async_copy(out_buf.at[rows], out_hbm.at[rows], sems.at[i])
        copy.start()
        copies.append(copy)
    for copy in copies:
        copy.wait()


def outbox(pick, middle, gain):
    slots, tokens = pick.shape
    width = middle.shape[1]
    count = 4
    return pl.pallas_call(
        functools.partial(outbox_kernel, count),
        in_specs=[pl.BlockSpec(memory_space=pltpu.VMEM)] * 3,
        out_specs=pl.BlockSpec(memory_space=pltpu.HBM),
        out_shape=jax.ShapeDtypeStruct((slots, width), BF16),
        scratch_shapes=[
            pltpu.VMEM((tokens, width), BF16),
            pltpu.VMEM((slots, width), BF16),
            pltpu.SemaphoreType.DMA((count,)),
        ],
        name="outbox",
        cost_estimate=pl.CostEstimate(
            flops=2 * slots * tokens * width, bytes_accessed=2 * slots * width, transcendentals=0
        ),
    )(pick, middle, gain)


def experts_kernel(
    count, x_hbm, gate_hbm, up_hbm, down_hbm, out_hbm, x_buf, gate_buf, up_buf, down_buf, out_buf,
    x_sems, weight_sems, out_sems
):
    rows = blocks(x_buf.shape[0], count)
    low, high = blocks(gate_buf.shape[0], 2)
    depth = gate_buf.shape[0] // 2
    copy = pltpu.make_async_copy
    x_in = [copy(x_hbm.at[r], x_buf.at[r], x_sems.at[i]) for i, r in enumerate(rows)]
    weights_in = [
        copy(gate_hbm.at[low], gate_buf.at[low], weight_sems.at[0]),
        copy(gate_hbm.at[high], gate_buf.at[high], weight_sems.at[1]),
        copy(up_hbm, up_buf, weight_sems.at[2]),
        copy(down_hbm, down_buf, weight_sems.at[3]),
    ]
    for each in [x_in[0], *weights_in[:3], *x_in[1:], weights_in[3]]:
        each.start()
    sent = []
    for i, r in enumerate(rows):
        x_in[i].wait()
        x = x_buf[r, :]
        if i == 0:
            weights_in[0].wait()
            gate = matmul(x[:, :depth], gate_buf[low, :])
            weights_in[1].wait()
            gate = gate + matmul(x[:, depth:], gate_buf[high, :])
            weights_in[2].wait()
        else:
            gate = matmul(x, gate_buf[...])
        up = matmul(x, up_buf[...])
        hidden = (gate / (1.0 + jnp.exp(-gate)) * up).astype(BF16)
        if i == 0:
            weights_in[3].wait()
        out_buf[r, :] = matmul(hidden, down_buf[...]).astype(BF16)
        out = copy(out_buf.at[r], out_hbm.at[r], out_sems.at[i])
        out.start()
        sent.append(out)
    for out in sent:
        out.wait()


def experts(x, w_gate, w_up, w_down):
    slots, width = x.shape
    inner = w_gate.shape[1]
    count = 4
    return pl.pallas_call(
        functools.partial(experts_kernel, count),
        in_specs=[pl.BlockSpec(memory_space=pltpu.HBM)] * 4,
        out_specs=pl.BlockSpec(memory_space=pltpu.HBM),
        out_shape=jax.ShapeDtypeStruct(x.shape, BF16),
        scratch_shapes=[pltpu.VMEM(a.shape, BF16) for a in (x, w_gate, w_up, w_down, x)]
        + [pltpu.SemaphoreType.DMA((n,)) for n in (count, 4, count)],
        compiler_params=pltpu.CompilerParams(vmem_limit_bytes=48 << 20),
        name="experts",
        cost_estimate=pl.CostEstimate(
            flops=6 * slots * width * inner,
            bytes_accessed=4 * slots * width + 6 * width * inner,
            transcendentals=slots * inner,
        ),
    )(x, w_gate, w_up, w_down)


def combine_kernel(mix_ref, middle_ref, returned_ref, out_ref):
    mixture = matmul(mix_ref[...], returned_ref[...])
    tokens = middle_ref.shape[0]
    mixture = mixture[:tokens] + mixture[tokens:]
    out_ref[...] = (middle_ref[...].astype(F32) + mixture).astype(BF16)


def combine(mix, middle, returned):
    count, width = returned.shape
    tokens = middle.shape[0]
    cols = width // 2
    return pl.pallas_call(
        combine_kernel,
        grid=(2,),
        in_specs=[
            pl.BlockSpec(mix.shape, lambda i: (0, 0)),
            pl.BlockSpec((tokens, cols), lambda i: (0, i)),
            pl.BlockSpec((count, cols), lambda i: (0, i)),
        ],
        out_specs=pl.BlockSpec((tokens, cols), lambda i: (0, i)),
        out_shape=jax.ShapeDtypeStruct(middle.shape, BF16),
        name="combine",
        cost_estimate=pl.CostEstimate(
            flops=4 * tokens * count * width, bytes_accessed=2 * count * width, transcendentals=0
        ),
    )(mix, middle, returned)


def slot_table(routes, expert_count, capacity):
    tokens = routes.shape[0]
    onehot = routes[:, :, None] == jnp.arange(expert_count, dtype=jnp.int32)[None, None, :]
    used = jnp.any(onehot, axis=1).astype(BF16)
    earlier = jnp.asarray(np.tril(np.ones((tokens, tokens)), -1), BF16)
    rank = matmul(earlier, used)
    rank = jnp.sum(jnp.where(onehot, rank[:, None, :], 0.0), axis=2).astype(jnp.int32)
    return routes * capacity + rank


def gather_plan(slots, gates, slot_count):
    index = jnp.arange(slot_count, dtype=jnp.int32)
    slots_t = slots.T
    pick = index[:, None] == slots_t[0][None, :]
    mix = jnp.where(index[None, :] == slots[:, :1], gates[:, :1], 0.0)
    for k in range(1, slots.shape[1]):
        pick = pick | (index[:, None] == slots_t[k][None, :])
        mix = jnp.where(index[None, :] == slots[:, k : k + 1], gates[:, k : k + 1], mix)
    high = lax.reduce_precision(mix, 8, 7)
    return pick.astype(BF16), jnp.concatenate([high, mix - high], axis=0).astype(BF16)


def shift(x, by, size):
    return lax.ppermute(x, "req", [(i, (i + by) % size) for i in range(size)])


def body(
    residual,
    q_proj,
    kv_proj,
    q_gain,
    k_gain,
    cache_k,
    cache_v,
    cache_len,
    parents,
    accepted_leaf,
    o_weight,
    post_gain,
    routes,
    route_gates,
    w_gate,
    w_up,
    w_down,
):
    tok_rows, model_width = residual.shape
    req_size = lax.axis_size("req")
    exp_size = lax.axis_size("exp")
    expert_count = req_size * exp_size
    top_count = routes.shape[1]
    capacity = max(2, 2 * tok_rows * top_count // expert_count)
    slot_count = expert_count * capacity

    attend = functools.partial(
        attention,
        cache_len,
        accepted_leaf,
        parents,
        q_gain,
        k_gain,
        q_proj,
        kv_proj,
        cache_k[0],
        cache_v[0],
    )
    left, left_keys, *made = attend(0, None)
    right, right_keys = attend(1, made)
    new_keys = append(cache_len, made[3], cache_k[0], [left_keys, right_keys])
    new_values = append(cache_len, made[3], cache_v[0], [kv_proj])
    slots = slot_table(routes, expert_count, capacity)
    pick, mix = gather_plan(slots, route_gates, slot_count)

    inner = left.shape[1]
    up_left, down_left = shift(left, -1, req_size), shift(left, 1, req_size)
    up_right, down_right = shift(right, -1, req_size), shift(right, 1, req_size)
    far_left = shift(up_left, -1, req_size)
    far_right = shift(down_right, 1, req_size)

    def project(a, b):
        return (matmul(a, o_weight[:inner]) + matmul(b, o_weight[inner:])).astype(BF16)

    own = project(left, right)
    near_up = project(up_left, up_right)
    near_down = project(down_left, down_right)
    from_up = shift(near_up, 1, req_size)
    from_down = shift(near_down, -1, req_size)
    from_far = shift(project(far_left, far_right), 2, req_size)
    pieces = [own, from_down, from_far, from_up]
    at = lax.axis_index("req").astype(jnp.int32)
    columns = []
    for j in range(req_size):
        step = lax.rem(j - at + req_size, req_size)
        column = pieces[0]
        for s in range(1, req_size):
            column = jnp.where(step == s, pieces[s], column)
        columns.append(column)
    projected = jnp.concatenate(columns, axis=1).astype(F32)
    middle = (residual.astype(F32) + projected).astype(BF16)

    def swap(x):
        return lax.all_to_all(
            x.reshape(expert_count, capacity, model_width),
            ("req", "exp"),
            split_axis=0,
            concat_axis=0,
            tiled=True,
        ).reshape(slot_count, model_width)

    arrived = swap(outbox(pick, middle, post_gain[None]))
    returned = swap(experts(arrived, w_gate[0], w_up[0], w_down[0]))
    hidden_out = combine(mix, middle, returned)
    return (hidden_out, new_keys[None], new_values[None])


def solution(mesh):
    placed = (
        P(("req", "exp"), None),
        P(("req", "exp"), None),
        P(("req", "exp"), None),
        P(),
        P(),
        P(("req", "exp"), None, None),
        P(("req", "exp"), None, None),
        P(("req", "exp")),
        P(("req", "exp"), None),
        P(("req", "exp")),
        P(None, "req"),
        P(),
        P(("req", "exp"), None),
        P(("req", "exp"), None),
        P(("req", "exp"), None, None),
        P(("req", "exp"), None, None),
        P(("req", "exp"), None, None),
    )
    return jax.shard_map(
        body,
        mesh=mesh,
        in_specs=placed,
        out_specs=(
            P(("req", "exp"), None),
            P(("req", "exp"), None, None),
            P(("req", "exp"), None, None),
        ),
        check_vma=False,
    )
```

```python
import functools

import jax
import jax.numpy as jnp
import numpy as np
from jax import lax
from jax.experimental import pallas as pl
from jax.experimental.pallas import tpu as pltpu
from jax.sharding import PartitionSpec as P


HEADS = 32
KV_HEADS = 4
WINDOW = 512
SINKS = 4

ROPE_BASE = 1000000.0
NORM_EPS = 1e-06
MASKED = -1e30

F32 = jnp.float32
BF16 = jnp.bfloat16


def matmul(a, b):
    return jnp.dot(a, b, preferred_element_type=F32)


def contract(a, b, dims_a, dims_b):
    return lax.dot_general(a, b, (((dims_a,), (dims_b,)), ((), ())), preferred_element_type=F32)


def iota(shape, axis):
    return lax.broadcasted_iota(jnp.int32, shape, axis)


def tables(length, leaf, parents_ref, freq_ref, span, slots, patch):
    draft = parents_ref.shape[1]
    width = freq_ref.shape[1]
    child = iota((draft, draft), 1)
    node = iota((draft, draft), 0)
    eye = (child == node).astype(F32)
    links = (eye + (parents_ref[...] == node).astype(F32)).astype(BF16)
    for _ in range((draft - 1).bit_length()):
        links = jnp.minimum(matmul(links, links), 1.0).astype(BF16)
    closure = contract(links, eye.astype(BF16), 0, 0)
    depth = jnp.sum(closure, axis=1, keepdims=True) - 1.0
    angle = (length.astype(F32) + depth) * freq_ref[...]
    sine = jnp.sin(angle)
    sine = jnp.where(iota((draft, width), 1) < width // 2, -sine, sine)
    head = iota((draft, width - draft), 1)
    first = jnp.minimum(jnp.maximum(length - WINDOW, 0) // 16 * 16, slots - span)
    seen = (head < SINKS) & (head < length) & (head < first)
    tree = jnp.concatenate(
        [jnp.where(closure > 0.5, 0.0, MASKED), jnp.where(seen, 0.0, MASKED)], axis=1
    )
    chosen = (iota((8, draft), 1) == leaf).astype(BF16)
    accepted = matmul(chosen, closure.astype(BF16))[:1]
    depths = contract(jnp.ones((8, draft), BF16), closure.astype(BF16), 1, 1)[:1] - 1.0
    row = iota((patch, draft), 0) + patch_start(length, slots, patch) - length
    place = ((row == depths.astype(jnp.int32)) & (accepted > 0.5)).astype(BF16)
    return jnp.cos(angle), sine, tree, place


def patch_start(length, slots, patch):
    return jnp.minimum(length // 16 * 16, slots - patch)


def attention_kernel(opening, span, *refs):
    length_ref, leaf_ref, q_gain_ref, k_gain_ref, q_ref, k_ref, v_ref, cache_k_ref, cache_v_ref = refs[:9]
    refs = refs[9:]
    if opening:
        parents_ref, freq_ref, out_ref, key_ref, cos_ref, sin_ref, tree_ref, place_ref = refs
    else:
        cos_ref, sin_ref, tree_ref, out_ref, key_ref = refs
    draft = k_ref.shape[0]
    width = k_ref.shape[1]
    slots = cache_k_ref.shape[0]
    group = q_ref.shape[1] // width
    length = length_ref[0]

    if opening:

        @pl.when(pl.program_id(0) == 0)
        def _():
            made = tables(
                length, leaf_ref[0], parents_ref, freq_ref, span, slots, place_ref.shape[0]
            )
            for ref, table in zip((cos_ref, sin_ref, tree_ref, place_ref), made):
                ref[...] = table

    cosine = cos_ref[...]
    sine = sin_ref[...]

    def turned(x, gain):
        x = x * lax.rsqrt(jnp.mean(x * x, axis=-1, keepdims=True) + NORM_EPS) * gain
        return x, pltpu.roll(x, width // 2, axis=1)

    k_new, k_swapped = turned(k_ref[...].astype(F32), k_gain_ref[...])
    k_new = (k_new * cosine + k_swapped * sine).astype(BF16)
    key_ref[...] = k_new
    queries = q_ref[...].astype(F32)
    queries = jnp.concatenate(
        [queries[:, h * width : (h + 1) * width] for h in range(group)], axis=0
    )
    queries, q_swapped = turned(queries, q_gain_ref[...])
    shape = (group, draft, width)
    queries = (
        queries.reshape(shape) * cosine[None] + q_swapped.reshape(shape) * sine[None]
    ).reshape(group * draft, width).astype(BF16)

    first = jnp.minimum(jnp.maximum(length - WINDOW, 0) // 16 * 16, slots - span)
    first = pl.multiple_of(first, 16)
    pad = jnp.zeros((width - draft - 16, width), BF16)
    keys = cache_k_ref[pl.ds(first, span), :]
    values = cache_v_ref[pl.ds(first, span), :]
    own_keys = jnp.concatenate([k_new, cache_k_ref[:16, :], pad], axis=0)
    own_values = jnp.concatenate([v_ref[...], cache_v_ref[:16, :], pad], axis=0)
    slot = iota((1, span), 1) + first
    seen = (slot < length) & ((slot < SINKS) | (slot >= length - WINDOW))
    far = contract(queries, keys, 1, 1) + jnp.where(seen, 0.0, MASKED)
    near = contract(queries, own_keys, 1, 1).reshape(shape) + tree_ref[...][None]
    near = near.reshape(group * draft, width)
    top = jnp.maximum(
        jnp.max(far, axis=-1, keepdims=True), jnp.max(near, axis=-1, keepdims=True)
    )
    scale = float(width) ** -0.5 * float(np.log2(np.e))
    far = jnp.exp2((far - top) * scale)
    near = jnp.exp2((near - top) * scale)
    total = jnp.sum(far, axis=-1, keepdims=True) + jnp.sum(near, axis=-1, keepdims=True)
    mixed = matmul(far.astype(BF16), values) + matmul(near.astype(BF16), own_values)
    mixed = (mixed / total).astype(BF16)
    for h in range(group):
        out_ref[:, h * width : (h + 1) * width] = mixed[h * draft : (h + 1) * draft]


def attention(length, leaf, parents, q_gain, k_gain, q_proj, kv_proj, cache_k, cache_v, at, made):
    draft = q_proj.shape[0]
    width = q_gain.shape[0]
    slots = cache_k.shape[0]
    span = min(slots, WINDOW + 128)
    per_group = HEADS // KV_HEADS * width
    groups = KV_HEADS // 2
    base = at * groups
    smem = pl.BlockSpec(memory_space=pltpu.SMEM)
    whole = lambda shape: pl.BlockSpec(shape, lambda g: (0, 0))
    table = jax.ShapeDtypeStruct((draft, width), F32)
    patch = draft + 16
    tables_shape = [table] * 3 + [jax.ShapeDtypeStruct((patch, draft), BF16)]
    in_specs = [
        smem,
        smem,
        whole((1, width)),
        whole((1, width)),
        pl.BlockSpec((draft, per_group), lambda g: (0, g + base)),
        pl.BlockSpec((draft, width), lambda g: (0, g + base)),
        pl.BlockSpec((draft, width), lambda g: (0, g + base + KV_HEADS)),
        pl.BlockSpec((slots, width), lambda g: (0, g + base)),
        pl.BlockSpec((slots, width), lambda g: (0, g + base)),
    ]
    out_specs = [
        pl.BlockSpec((draft, per_group), lambda g: (0, g)),
        pl.BlockSpec((draft, width), lambda g: (0, g)),
    ]
    out_shape = [
        jax.ShapeDtypeStruct((draft, per_group * groups), BF16),
        jax.ShapeDtypeStruct((draft, width * groups), BF16),
    ]
    operands = [length, leaf, q_gain[None], k_gain[None], q_proj, kv_proj, kv_proj, cache_k, cache_v]
    if made is None:
        half = width // 2
        freq = ROPE_BASE ** (-(np.arange(half) * 2.0) / width)
        freq = jnp.asarray(np.concatenate([freq, freq])[None, :], F32)
        operands += [parents, freq]
        in_specs += [whole((1, draft)), whole((1, width))]
        out_specs += [whole(t.shape) for t in tables_shape]
        out_shape += tables_shape
    else:
        operands += made[:3]
        in_specs += [whole(t.shape) for t in made[:3]]
    return pl.pallas_call(
        functools.partial(attention_kernel, made is None, span),
        grid=(groups,),
        in_specs=in_specs,
        out_specs=out_specs,
        out_shape=out_shape,
        cost_estimate=pl.CostEstimate(
            flops=2 * HEADS * draft * (span + width) * width,
            bytes_accessed=2 << 20,
            transcendentals=HEADS // 2 * draft * (span + width),
        ),
    )(*operands)


def append_kernel(length_ref, place_ref, cache_ref, *rest):
    new_ref = rest[-1]
    patch = place_ref.shape[0]
    slots = cache_ref.shape[0]
    at = pl.multiple_of(patch_start(length_ref[0], slots, patch), 16)
    place = place_ref[...]
    taken = jnp.sum(place.astype(F32), axis=1, keepdims=True) > 0.5
    rows = pl.ds(at, patch)
    fresh = rest[0][...]
    if len(rest) > 2:
        fresh = jnp.where(pl.program_id(0) == 0, fresh, rest[1][...])
    new_ref[...] = cache_ref[...]
    put = matmul(place, fresh).astype(BF16)
    new_ref[rows, :] = jnp.where(taken, put, cache_ref[rows, :])


def append(length, place, cache, fresh):
    slots, width = cache.shape
    draft = place.shape[1]
    cols = width // 2
    whole = lambda x: pl.BlockSpec(x.shape, lambda g: (0, 0))
    cache_spec = pl.BlockSpec((slots, cols), lambda g: (0, g))
    last = [pl.BlockSpec((draft, cols), lambda g: (0, g + 2))]
    return pl.pallas_call(
        append_kernel,
        grid=(2,),
        in_specs=[pl.BlockSpec(memory_space=pltpu.SMEM), whole(place), cache_spec]
        + (last if len(fresh) == 1 else [whole(x) for x in fresh]),
        out_specs=cache_spec,
        out_shape=jax.ShapeDtypeStruct(cache.shape, BF16),
        cost_estimate=pl.CostEstimate(
            flops=4 * place.shape[0] * draft * cols,
            bytes_accessed=4 * slots * width,
            transcendentals=0,
        ),
    )(length, place, cache, *fresh)


def blocks(total, count):
    return [pl.ds(i * (total // count), total // count) for i in range(count)]


def outbox_kernel(count, pick_ref, middle_ref, gain_ref, out_hbm, normed_ref, out_buf, sems):
    middle = middle_ref[...].astype(F32)
    power = jnp.mean(middle * middle, axis=-1, keepdims=True)
    normed_ref[...] = (middle * lax.rsqrt(power + NORM_EPS) * gain_ref[...]).astype(BF16)
    copies = []
    for i, rows in enumerate(blocks(out_buf.shape[0], count)):
        out_buf[rows, :] = matmul(pick_ref[rows, :], normed_ref[...]).astype(BF16)
        copy = pltpu.make_async_copy(out_buf.at[rows], out_hbm.at[rows], sems.at[i])
        copy.start()
        copies.append(copy)
    for copy in copies:
        copy.wait()


def outbox(pick, middle, gain):
    slots, tokens = pick.shape
    width = middle.shape[1]
    count = 4
    return pl.pallas_call(
        functools.partial(outbox_kernel, count),
        in_specs=[pl.BlockSpec(memory_space=pltpu.VMEM)] * 3,
        out_specs=pl.BlockSpec(memory_space=pltpu.HBM),
        out_shape=jax.ShapeDtypeStruct((slots, width), BF16),
        scratch_shapes=[
            pltpu.VMEM((tokens, width), BF16),
            pltpu.VMEM((slots, width), BF16),
            pltpu.SemaphoreType.DMA((count,)),
        ],
        name="outbox",
        cost_estimate=pl.CostEstimate(
            flops=2 * slots * tokens * width, bytes_accessed=2 * slots * width, transcendentals=0
        ),
    )(pick, middle, gain)


def experts_kernel(
    count, x_hbm, gate_hbm, up_hbm, down_hbm, out_hbm, x_buf, gate_buf, up_buf, down_buf, out_buf,
    x_sems, weight_sems, out_sems
):
    rows = blocks(x_buf.shape[0], count)
    low, high = blocks(gate_buf.shape[0], 2)
    depth = gate_buf.shape[0] // 2
    copy = pltpu.make_async_copy
    x_in = [copy(x_hbm.at[r], x_buf.at[r], x_sems.at[i]) for i, r in enumerate(rows)]
    weights_in = [
        copy(gate_hbm.at[low], gate_buf.at[low], weight_sems.at[0]),
        copy(gate_hbm.at[high], gate_buf.at[high], weight_sems.at[1]),
        copy(up_hbm, up_buf, weight_sems.at[2]),
        copy(down_hbm, down_buf, weight_sems.at[3]),
    ]
    for each in [x_in[0], *weights_in[:3], *x_in[1:], weights_in[3]]:
        each.start()
    sent = []
    for i, r in enumerate(rows):
        x_in[i].wait()
        x = x_buf[r, :]
        if i == 0:
            weights_in[0].wait()
            gate = matmul(x[:, :depth], gate_buf[low, :])
            weights_in[1].wait()
            gate = gate + matmul(x[:, depth:], gate_buf[high, :])
            weights_in[2].wait()
        else:
            gate = matmul(x, gate_buf[...])
        up = matmul(x, up_buf[...])
        hidden = (gate / (1.0 + jnp.exp(-gate)) * up).astype(BF16)
        if i == 0:
            weights_in[3].wait()
        out_buf[r, :] = matmul(hidden, down_buf[...]).astype(BF16)
        out = copy(out_buf.at[r], out_hbm.at[r], out_sems.at[i])
        out.start()
        sent.append(out)
    for out in sent:
        out.wait()


def experts(x, w_gate, w_up, w_down):
    slots, width = x.shape
    inner = w_gate.shape[1]
    count = 4
    return pl.pallas_call(
        functools.partial(experts_kernel, count),
        in_specs=[pl.BlockSpec(memory_space=pltpu.HBM)] * 4,
        out_specs=pl.BlockSpec(memory_space=pltpu.HBM),
        out_shape=jax.ShapeDtypeStruct(x.shape, BF16),
        scratch_shapes=[pltpu.VMEM(a.shape, BF16) for a in (x, w_gate, w_up, w_down, x)]
        + [pltpu.SemaphoreType.DMA((n,)) for n in (count, 4, count)],
        compiler_params=pltpu.CompilerParams(vmem_limit_bytes=48 << 20),
        name="experts",
        cost_estimate=pl.CostEstimate(
            flops=6 * slots * width * inner,
            bytes_accessed=4 * slots * width + 6 * width * inner,
            transcendentals=slots * inner,
        ),
    )(x, w_gate, w_up, w_down)


def combine_kernel(mix_ref, middle_ref, returned_ref, out_ref):
    mixture = matmul(mix_ref[...], returned_ref[...])
    tokens = middle_ref.shape[0]
    mixture = mixture[:tokens] + mixture[tokens:]
    out_ref[...] = (middle_ref[...].astype(F32) + mixture).astype(BF16)


def combine(mix, middle, returned):
    count, width = returned.shape
    tokens = middle.shape[0]
    cols = width // 2
    return pl.pallas_call(
        combine_kernel,
        grid=(2,),
        in_specs=[
            pl.BlockSpec(mix.shape, lambda i: (0, 0)),
            pl.BlockSpec((tokens, cols), lambda i: (0, i)),
            pl.BlockSpec((count, cols), lambda i: (0, i)),
        ],
        out_specs=pl.BlockSpec((tokens, cols), lambda i: (0, i)),
        out_shape=jax.ShapeDtypeStruct(middle.shape, BF16),
        name="combine",
        cost_estimate=pl.CostEstimate(
            flops=4 * tokens * count * width, bytes_accessed=2 * count * width, transcendentals=0
        ),
    )(mix, middle, returned)


def slot_table(routes, expert_count, capacity):
    tokens = routes.shape[0]
    onehot = routes[:, :, None] == jnp.arange(expert_count, dtype=jnp.int32)[None, None, :]
    used = jnp.any(onehot, axis=1).astype(BF16)
    earlier = jnp.asarray(np.tril(np.ones((tokens, tokens)), -1), BF16)
    rank = matmul(earlier, used)
    rank = jnp.sum(jnp.where(onehot, rank[:, None, :], 0.0), axis=2).astype(jnp.int32)
    return routes * capacity + rank


def gather_plan(slots, gates, slot_count):
    index = jnp.arange(slot_count, dtype=jnp.int32)
    slots_t = slots.T
    pick = index[:, None] == slots_t[0][None, :]
    mix = jnp.where(index[None, :] == slots[:, :1], gates[:, :1], 0.0)
    for k in range(1, slots.shape[1]):
        pick = pick | (index[:, None] == slots_t[k][None, :])
        mix = jnp.where(index[None, :] == slots[:, k : k + 1], gates[:, k : k + 1], mix)
    high = lax.reduce_precision(mix, 8, 7)
    return pick.astype(BF16), jnp.concatenate([high, mix - high], axis=0).astype(BF16)


def shift(x, by, size):
    return lax.ppermute(x, "req", [(i, (i + by) % size) for i in range(size)])


def body(
    residual,
    q_proj,
    kv_proj,
    q_gain,
    k_gain,
    cache_k,
    cache_v,
    cache_len,
    parents,
    accepted_leaf,
    o_weight,
    post_gain,
    routes,
    route_gates,
    w_gate,
    w_up,
    w_down,
):
    tok_rows, model_width = residual.shape
    req_size = lax.axis_size("req")
    exp_size = lax.axis_size("exp")
    expert_count = req_size * exp_size
    top_count = routes.shape[1]
    capacity = max(2, 2 * tok_rows * top_count // expert_count)
    slot_count = expert_count * capacity

    attend = functools.partial(
        attention,
        cache_len,
        accepted_leaf,
        parents,
        q_gain,
        k_gain,
        q_proj,
        kv_proj,
        cache_k[0],
        cache_v[0],
    )
    left, left_keys, *made = attend(0, None)
    right, right_keys = attend(1, made)
    new_keys = append(cache_len, made[3], cache_k[0], [left_keys, right_keys])
    new_values = append(cache_len, made[3], cache_v[0], [kv_proj])
    slots = slot_table(routes, expert_count, capacity)
    pick, mix = gather_plan(slots, route_gates, slot_count)

    inner = left.shape[1]
    cut = inner // 2
    rights = (right[:, :cut], right[:, cut:])
    up_left, down_left = shift(left, -1, req_size), shift(left, 1, req_size)
    up_rights, down_rights = [], []
    for x in rights:
        down_rights.append(shift(x, 1, req_size))
        up_rights.append(shift(x, -1, req_size))
    far_left = shift(up_left, -1, req_size)
    far_rights = []
    for x in down_rights:
        far_rights.append(shift(x, 1, req_size))

    def project(a, b):
        product = matmul(a, o_weight[:inner])
        for i, x in enumerate(b):
            product = product + matmul(x, o_weight[inner + i * cut : inner + (i + 1) * cut])
        return product.astype(BF16)

    own = matmul(left, o_weight[:inner]) + matmul(right, o_weight[inner:])
    own = own.astype(BF16)
    near_up = project(up_left, up_rights)
    near_down = project(down_left, down_rights)
    from_up = shift(near_up, 1, req_size)
    from_down = shift(near_down, -1, req_size)
    from_far = shift(project(far_left, far_rights), 2, req_size)
    pieces = [own, from_down, from_far, from_up]
    at = lax.axis_index("req").astype(jnp.int32)
    columns = []
    for j in range(req_size):
        step = lax.rem(j - at + req_size, req_size)
        column = pieces[0]
        for s in range(1, req_size):
            column = jnp.where(step == s, pieces[s], column)
        columns.append(column)
    projected = jnp.concatenate(columns, axis=1).astype(F32)
    middle = (residual.astype(F32) + projected).astype(BF16)

    def swap(x):
        return lax.all_to_all(
            x.reshape(expert_count, capacity, model_width),
            ("req", "exp"),
            split_axis=0,
            concat_axis=0,
            tiled=True,
        ).reshape(slot_count, model_width)

    arrived = swap(outbox(pick, middle, post_gain[None]))
    returned = swap(experts(arrived, w_gate[0], w_up[0], w_down[0]))
    hidden_out = combine(mix, middle, returned)
    return (hidden_out, new_keys[None], new_values[None])


def solution(mesh):
    placed = (
        P(("req", "exp"), None),
        P(("req", "exp"), None),
        P(("req", "exp"), None),
        P(),
        P(),
        P(("req", "exp"), None, None),
        P(("req", "exp"), None, None),
        P(("req", "exp")),
        P(("req", "exp"), None),
        P(("req", "exp")),
        P(None, "req"),
        P(),
        P(("req", "exp"), None),
        P(("req", "exp"), None),
        P(("req", "exp"), None, None),
        P(("req", "exp"), None, None),
        P(("req", "exp"), None, None),
    )
    return jax.shard_map(
        body,
        mesh=mesh,
        in_specs=placed,
        out_specs=(
            P(("req", "exp"), None),
            P(("req", "exp"), None, None),
            P(("req", "exp"), None, None),
        ),
        check_vma=False,
    )
```

```python
import functools

import jax
import jax.numpy as jnp
import numpy as np
from jax import lax
from jax.experimental import pallas as pl
from jax.experimental.pallas import tpu as pltpu
from jax.sharding import PartitionSpec as P


HEADS = 32
KV_HEADS = 4
WINDOW = 512
SINKS = 4

ROPE_BASE = 1000000.0
NORM_EPS = 1e-06
MASKED = -1e30

F32 = jnp.float32
BF16 = jnp.bfloat16


def matmul(a, b):
    return jnp.dot(a, b, preferred_element_type=F32)


def contract(a, b, dims_a, dims_b):
    return lax.dot_general(a, b, (((dims_a,), (dims_b,)), ((), ())), preferred_element_type=F32)


def iota(shape, axis):
    return lax.broadcasted_iota(jnp.int32, shape, axis)


def tables(length, leaf, parents_ref, freq_ref, span, slots, patch):
    draft = parents_ref.shape[1]
    width = freq_ref.shape[1]
    child = iota((draft, draft), 1)
    node = iota((draft, draft), 0)
    eye = (child == node).astype(F32)
    links = (eye + (parents_ref[...] == node).astype(F32)).astype(BF16)
    for _ in range((draft - 1).bit_length()):
        links = jnp.minimum(matmul(links, links), 1.0).astype(BF16)
    closure = contract(links, eye.astype(BF16), 0, 0)
    depth = jnp.sum(closure, axis=1, keepdims=True) - 1.0
    angle = (length.astype(F32) + depth) * freq_ref[...]
    sine = jnp.sin(angle)
    sine = jnp.where(iota((draft, width), 1) < width // 2, -sine, sine)
    head = iota((draft, width - draft), 1)
    first = jnp.minimum(jnp.maximum(length - WINDOW, 0) // 16 * 16, slots - span)
    seen = (head < SINKS) & (head < length) & (head < first)
    tree = jnp.concatenate(
        [jnp.where(closure > 0.5, 0.0, MASKED), jnp.where(seen, 0.0, MASKED)], axis=1
    )
    chosen = (iota((8, draft), 1) == leaf).astype(BF16)
    accepted = matmul(chosen, closure.astype(BF16))[:1]
    depths = contract(jnp.ones((8, draft), BF16), closure.astype(BF16), 1, 1)[:1] - 1.0
    row = iota((patch, draft), 0) + patch_start(length, slots, patch) - length
    place = ((row == depths.astype(jnp.int32)) & (accepted > 0.5)).astype(BF16)
    return jnp.cos(angle), sine, tree, place


def patch_start(length, slots, patch):
    return jnp.minimum(length // 16 * 16, slots - patch)


def attention_kernel(opening, span, *refs):
    length_ref, leaf_ref, q_gain_ref, k_gain_ref, q_ref, k_ref, v_ref, cache_k_ref, cache_v_ref = refs[:9]
    refs = refs[9:]
    if opening:
        parents_ref, freq_ref, out_ref, key_ref, cos_ref, sin_ref, tree_ref, place_ref = refs
    else:
        cos_ref, sin_ref, tree_ref, out_ref, key_ref = refs
    draft = k_ref.shape[0]
    width = k_ref.shape[1]
    slots = cache_k_ref.shape[0]
    group = q_ref.shape[1] // width
    length = length_ref[0]

    if opening:

        @pl.when(pl.program_id(0) == 0)
        def _():
            made = tables(
                length, leaf_ref[0], parents_ref, freq_ref, span, slots, place_ref.shape[0]
            )
            for ref, table in zip((cos_ref, sin_ref, tree_ref, place_ref), made):
                ref[...] = table

    cosine = cos_ref[...]
    sine = sin_ref[...]

    def turned(x, gain):
        x = x * lax.rsqrt(jnp.mean(x * x, axis=-1, keepdims=True) + NORM_EPS) * gain
        return x, pltpu.roll(x, width // 2, axis=1)

    k_new, k_swapped = turned(k_ref[...].astype(F32), k_gain_ref[...])
    k_new = (k_new * cosine + k_swapped * sine).astype(BF16)
    key_ref[...] = k_new
    queries = q_ref[...].astype(F32)
    queries = jnp.concatenate(
        [queries[:, h * width : (h + 1) * width] for h in range(group)], axis=0
    )
    queries, q_swapped = turned(queries, q_gain_ref[...])
    shape = (group, draft, width)
    queries = (
        queries.reshape(shape) * cosine[None] + q_swapped.reshape(shape) * sine[None]
    ).reshape(group * draft, width).astype(BF16)

    first = jnp.minimum(jnp.maximum(length - WINDOW, 0) // 16 * 16, slots - span)
    first = pl.multiple_of(first, 16)
    pad = jnp.zeros((width - draft - 16, width), BF16)
    keys = cache_k_ref[pl.ds(first, span), :]
    values = cache_v_ref[pl.ds(first, span), :]
    own_keys = jnp.concatenate([k_new, cache_k_ref[:16, :], pad], axis=0)
    own_values = jnp.concatenate([v_ref[...], cache_v_ref[:16, :], pad], axis=0)
    slot = iota((1, span), 1) + first
    seen = (slot < length) & ((slot < SINKS) | (slot >= length - WINDOW))
    far = contract(queries, keys, 1, 1) + jnp.where(seen, 0.0, MASKED)
    near = contract(queries, own_keys, 1, 1).reshape(shape) + tree_ref[...][None]
    near = near.reshape(group * draft, width)
    top = jnp.maximum(
        jnp.max(far, axis=-1, keepdims=True), jnp.max(near, axis=-1, keepdims=True)
    )
    scale = float(width) ** -0.5 * float(np.log2(np.e))
    far = jnp.exp2((far - top) * scale)
    near = jnp.exp2((near - top) * scale)
    total = jnp.sum(far, axis=-1, keepdims=True) + jnp.sum(near, axis=-1, keepdims=True)
    mixed = matmul(far.astype(BF16), values) + matmul(near.astype(BF16), own_values)
    mixed = (mixed / total).astype(BF16)
    for h in range(group):
        out_ref[:, h * width : (h + 1) * width] = mixed[h * draft : (h + 1) * draft]


def attention(length, leaf, parents, q_gain, k_gain, q_proj, kv_proj, cache_k, cache_v, at, made):
    draft = q_proj.shape[0]
    width = q_gain.shape[0]
    slots = cache_k.shape[0]
    span = min(slots, WINDOW + 128)
    per_group = HEADS // KV_HEADS * width
    groups = KV_HEADS // 2
    base = at * groups
    smem = pl.BlockSpec(memory_space=pltpu.SMEM)
    whole = lambda shape: pl.BlockSpec(shape, lambda g: (0, 0))
    table = jax.ShapeDtypeStruct((draft, width), F32)
    patch = draft + 16
    tables_shape = [table] * 3 + [jax.ShapeDtypeStruct((patch, draft), BF16)]
    in_specs = [
        smem,
        smem,
        whole((1, width)),
        whole((1, width)),
        pl.BlockSpec((draft, per_group), lambda g: (0, g + base)),
        pl.BlockSpec((draft, width), lambda g: (0, g + base)),
        pl.BlockSpec((draft, width), lambda g: (0, g + base + KV_HEADS)),
        pl.BlockSpec((slots, width), lambda g: (0, g + base)),
        pl.BlockSpec((slots, width), lambda g: (0, g + base)),
    ]
    out_specs = [
        pl.BlockSpec((draft, per_group), lambda g: (0, g)),
        pl.BlockSpec((draft, width), lambda g: (0, g)),
    ]
    out_shape = [
        jax.ShapeDtypeStruct((draft, per_group * groups), BF16),
        jax.ShapeDtypeStruct((draft, width * groups), BF16),
    ]
    operands = [length, leaf, q_gain[None], k_gain[None], q_proj, kv_proj, kv_proj, cache_k, cache_v]
    if made is None:
        half = width // 2
        freq = ROPE_BASE ** (-(np.arange(half) * 2.0) / width)
        freq = jnp.asarray(np.concatenate([freq, freq])[None, :], F32)
        operands += [parents, freq]
        in_specs += [whole((1, draft)), whole((1, width))]
        out_specs += [whole(t.shape) for t in tables_shape]
        out_shape += tables_shape
    else:
        operands += made[:3]
        in_specs += [whole(t.shape) for t in made[:3]]
    return pl.pallas_call(
        functools.partial(attention_kernel, made is None, span),
        grid=(groups,),
        in_specs=in_specs,
        out_specs=out_specs,
        out_shape=out_shape,
        cost_estimate=pl.CostEstimate(
            flops=2 * HEADS * draft * (span + width) * width,
            bytes_accessed=2 << 20,
            transcendentals=HEADS // 2 * draft * (span + width),
        ),
    )(*operands)


def append_kernel(length_ref, place_ref, cache_ref, *rest):
    new_ref = rest[-1]
    patch = place_ref.shape[0]
    slots = cache_ref.shape[0]
    at = pl.multiple_of(patch_start(length_ref[0], slots, patch), 16)
    place = place_ref[...]
    taken = jnp.sum(place.astype(F32), axis=1, keepdims=True) > 0.5
    rows = pl.ds(at, patch)
    fresh = rest[0][...]
    if len(rest) > 2:
        fresh = jnp.where(pl.program_id(0) == 0, fresh, rest[1][...])
    new_ref[...] = cache_ref[...]
    put = matmul(place, fresh).astype(BF16)
    new_ref[rows, :] = jnp.where(taken, put, cache_ref[rows, :])


def append(length, place, cache, fresh):
    slots, width = cache.shape
    draft = place.shape[1]
    cols = width // 2
    whole = lambda x: pl.BlockSpec(x.shape, lambda g: (0, 0))
    cache_spec = pl.BlockSpec((slots, cols), lambda g: (0, g))
    last = [pl.BlockSpec((draft, cols), lambda g: (0, g + 2))]
    return pl.pallas_call(
        append_kernel,
        grid=(2,),
        in_specs=[pl.BlockSpec(memory_space=pltpu.SMEM), whole(place), cache_spec]
        + (last if len(fresh) == 1 else [whole(x) for x in fresh]),
        out_specs=cache_spec,
        out_shape=jax.ShapeDtypeStruct(cache.shape, BF16),
        cost_estimate=pl.CostEstimate(
            flops=4 * place.shape[0] * draft * cols,
            bytes_accessed=4 * slots * width,
            transcendentals=0,
        ),
    )(length, place, cache, *fresh)


def blocks(total, count):
    return [pl.ds(i * (total // count), total // count) for i in range(count)]


def outbox_kernel(count, pick_ref, middle_ref, gain_ref, out_hbm, normed_ref, out_buf, sems):
    middle = middle_ref[...].astype(F32)
    power = jnp.mean(middle * middle, axis=-1, keepdims=True)
    normed_ref[...] = (middle * lax.rsqrt(power + NORM_EPS) * gain_ref[...]).astype(BF16)
    copies = []
    for i, rows in enumerate(blocks(out_buf.shape[0], count)):
        out_buf[rows, :] = matmul(pick_ref[rows, :], normed_ref[...]).astype(BF16)
        copy = pltpu.make_async_copy(out_buf.at[rows], out_hbm.at[rows], sems.at[i])
        copy.start()
        copies.append(copy)
    for copy in copies:
        copy.wait()


def outbox(pick, middle, gain):
    slots, tokens = pick.shape
    width = middle.shape[1]
    count = 8
    return pl.pallas_call(
        functools.partial(outbox_kernel, count),
        in_specs=[pl.BlockSpec(memory_space=pltpu.VMEM)] * 3,
        out_specs=pl.BlockSpec(memory_space=pltpu.HBM),
        out_shape=jax.ShapeDtypeStruct((slots, width), BF16),
        scratch_shapes=[
            pltpu.VMEM((tokens, width), BF16),
            pltpu.VMEM((slots, width), BF16),
            pltpu.SemaphoreType.DMA((count,)),
        ],
        name="outbox",
        cost_estimate=pl.CostEstimate(
            flops=2 * slots * tokens * width, bytes_accessed=2 * slots * width, transcendentals=0
        ),
    )(pick, middle, gain)


def experts_kernel(
    count, x_hbm, gate_hbm, up_hbm, down_hbm, out_hbm, x_buf, gate_buf, up_buf, down_buf, out_buf,
    x_sems, weight_sems, out_sems
):
    rows = blocks(x_buf.shape[0], count)
    low, high = blocks(gate_buf.shape[0], 2)
    depth = gate_buf.shape[0] // 2
    copy = pltpu.make_async_copy
    x_in = [copy(x_hbm.at[r], x_buf.at[r], x_sems.at[i]) for i, r in enumerate(rows)]
    weights_in = [
        copy(gate_hbm.at[low], gate_buf.at[low], weight_sems.at[0]),
        copy(gate_hbm.at[high], gate_buf.at[high], weight_sems.at[1]),
        copy(up_hbm, up_buf, weight_sems.at[2]),
        copy(down_hbm, down_buf, weight_sems.at[3]),
    ]
    for each in [x_in[0], *weights_in[:3], *x_in[1:], weights_in[3]]:
        each.start()
    sent = []
    held = []

    def finish(i):
        r = rows[i]
        if i == 0:
            weights_in[3].wait()
        out_buf[r, :] = matmul(held[i], down_buf[...]).astype(BF16)
        out = copy(out_buf.at[r], out_hbm.at[r], out_sems.at[i])
        out.start()
        sent.append(out)

    for i, r in enumerate(rows):
        x_in[i].wait()
        x = x_buf[r, :]
        if i == 0:
            weights_in[0].wait()
            gate = matmul(x[:, :depth], gate_buf[low, :])
            weights_in[1].wait()
            gate = gate + matmul(x[:, depth:], gate_buf[high, :])
            weights_in[2].wait()
        else:
            gate = matmul(x, gate_buf[...])
        up = matmul(x, up_buf[...])
        held.append((gate / (1.0 + jnp.exp(-gate)) * up).astype(BF16))
        if i:
            finish(i - 1)
    finish(len(rows) - 1)
    for out in sent:
        out.wait()


def experts(x, w_gate, w_up, w_down):
    slots, width = x.shape
    inner = w_gate.shape[1]
    count = 4
    return pl.pallas_call(
        functools.partial(experts_kernel, count),
        in_specs=[pl.BlockSpec(memory_space=pltpu.HBM)] * 4,
        out_specs=pl.BlockSpec(memory_space=pltpu.HBM),
        out_shape=jax.ShapeDtypeStruct(x.shape, BF16),
        scratch_shapes=[pltpu.VMEM(a.shape, BF16) for a in (x, w_gate, w_up, w_down, x)]
        + [pltpu.SemaphoreType.DMA((n,)) for n in (count, 4, count)],
        compiler_params=pltpu.CompilerParams(vmem_limit_bytes=43 << 20),
        name="experts",
        cost_estimate=pl.CostEstimate(
            flops=6 * slots * width * inner,
            bytes_accessed=4 * slots * width + 6 * width * inner,
            transcendentals=slots * inner,
        ),
    )(x, w_gate, w_up, w_down)


def combine_kernel(mix_ref, middle_ref, returned_ref, out_ref):
    mixture = matmul(mix_ref[...], returned_ref[...])
    tokens = middle_ref.shape[0]
    mixture = mixture[:tokens] + mixture[tokens:]
    out_ref[...] = (middle_ref[...].astype(F32) + mixture).astype(BF16)


def combine(mix, middle, returned):
    count, width = returned.shape
    tokens = middle.shape[0]
    cols = width // 2
    return pl.pallas_call(
        combine_kernel,
        grid=(2,),
        in_specs=[
            pl.BlockSpec(mix.shape, lambda i: (0, 0)),
            pl.BlockSpec((tokens, cols), lambda i: (0, i)),
            pl.BlockSpec((count, cols), lambda i: (0, i)),
        ],
        out_specs=pl.BlockSpec((tokens, cols), lambda i: (0, i)),
        out_shape=jax.ShapeDtypeStruct(middle.shape, BF16),
        name="combine",
        cost_estimate=pl.CostEstimate(
            flops=4 * tokens * count * width, bytes_accessed=2 * count * width, transcendentals=0
        ),
    )(mix, middle, returned)


def slot_table(routes, expert_count, capacity):
    tokens = routes.shape[0]
    onehot = routes[:, :, None] == jnp.arange(expert_count, dtype=jnp.int32)[None, None, :]
    used = jnp.any(onehot, axis=1).astype(BF16)
    earlier = jnp.asarray(np.tril(np.ones((tokens, tokens)), -1), BF16)
    rank = matmul(earlier, used)
    rank = jnp.sum(jnp.where(onehot, rank[:, None, :], 0.0), axis=2).astype(jnp.int32)
    return routes * capacity + rank


def gather_plan(slots, gates, slot_count):
    index = jnp.arange(slot_count, dtype=jnp.int32)
    slots_t = slots.T
    pick = index[:, None] == slots_t[0][None, :]
    mix = jnp.where(index[None, :] == slots[:, :1], gates[:, :1], 0.0)
    for k in range(1, slots.shape[1]):
        pick = pick | (index[:, None] == slots_t[k][None, :])
        mix = jnp.where(index[None, :] == slots[:, k : k + 1], gates[:, k : k + 1], mix)
    high = lax.reduce_precision(mix, 8, 7)
    return pick.astype(BF16), jnp.concatenate([high, mix - high], axis=0).astype(BF16)


def shift(x, by, size):
    return lax.ppermute(x, "req", [(i, (i + by) % size) for i in range(size)])


def body(
    residual,
    q_proj,
    kv_proj,
    q_gain,
    k_gain,
    cache_k,
    cache_v,
    cache_len,
    parents,
    accepted_leaf,
    o_weight,
    post_gain,
    routes,
    route_gates,
    w_gate,
    w_up,
    w_down,
):
    tok_rows, model_width = residual.shape
    req_size = lax.axis_size("req")
    exp_size = lax.axis_size("exp")
    expert_count = req_size * exp_size
    top_count = routes.shape[1]
    capacity = max(2, 2 * tok_rows * top_count // expert_count)
    slot_count = expert_count * capacity

    attend = functools.partial(
        attention,
        cache_len,
        accepted_leaf,
        parents,
        q_gain,
        k_gain,
        q_proj,
        kv_proj,
        cache_k[0],
        cache_v[0],
    )
    left, left_keys, *made = attend(0, None)
    right, right_keys = attend(1, made)
    new_keys = append(cache_len, made[3], cache_k[0], [left_keys, right_keys])
    new_values = append(cache_len, made[3], cache_v[0], [kv_proj])
    slots = slot_table(routes, expert_count, capacity)
    pick, mix = gather_plan(slots, route_gates, slot_count)

    inner = left.shape[1]
    up_left, down_left = shift(left, -1, req_size), shift(left, 1, req_size)
    up_right, down_right = shift(right, -1, req_size), shift(right, 1, req_size)
    far_left = shift(up_left, -1, req_size)
    far_right = shift(down_right, 1, req_size)

    def project(a, b):
        return (matmul(a, o_weight[:inner]) + matmul(b, o_weight[inner:])).astype(BF16)

    own = project(left, right)
    near_up = project(up_left, up_right)
    near_down = project(down_left, down_right)
    from_up = shift(near_up, 1, req_size)
    from_down = shift(near_down, -1, req_size)
    from_far = shift(project(far_left, far_right), 2, req_size)
    pieces = [own, from_down, from_far, from_up]
    at = lax.axis_index("req").astype(jnp.int32)
    columns = []
    for j in range(req_size):
        step = lax.rem(j - at + req_size, req_size)
        column = pieces[0]
        for s in range(1, req_size):
            column = jnp.where(step == s, pieces[s], column)
        columns.append(column)
    projected = jnp.concatenate(columns, axis=1).astype(F32)
    middle = (residual.astype(F32) + projected).astype(BF16)

    def swap(x):
        return lax.all_to_all(
            x.reshape(expert_count, capacity, model_width),
            ("req", "exp"),
            split_axis=0,
            concat_axis=0,
            tiled=True,
        ).reshape(slot_count, model_width)

    arrived = swap(outbox(pick, middle, post_gain[None]))
    returned = swap(experts(arrived, w_gate[0], w_up[0], w_down[0]))
    hidden_out = combine(mix, middle, returned)
    return (hidden_out, new_keys[None], new_values[None])


def solution(mesh):
    placed = (
        P(("req", "exp"), None),
        P(("req", "exp"), None),
        P(("req", "exp"), None),
        P(),
        P(),
        P(("req", "exp"), None, None),
        P(("req", "exp"), None, None),
        P(("req", "exp")),
        P(("req", "exp"), None),
        P(("req", "exp")),
        P(None, "req"),
        P(),
        P(("req", "exp"), None),
        P(("req", "exp"), None),
        P(("req", "exp"), None, None),
        P(("req", "exp"), None, None),
        P(("req", "exp"), None, None),
    )
    return jax.shard_map(
        body,
        mesh=mesh,
        in_specs=placed,
        out_specs=(
            P(("req", "exp"), None),
            P(("req", "exp"), None, None),
            P(("req", "exp"), None, None),
        ),
        check_vma=False,
    )
```
